512 devices in a mesh: col: 16 (over z, x_lo), row: 32 (over y, x_hi, core).
Axes of the slice: x: 4 (x_hi: 2, x_lo: 2; x = x_hi * 2 + x_lo), y: 8, z: 8, core: 2. Of those that a mesh axis runs over, the one named last changes fastest.
Arguments:
- inputs: bfloat16 [1024, 8192], P('row', 'col'), may hold values from -6 to 6
- grad_out: bfloat16 [1024, 8192], P('row', 'col'), may hold values from -6 to 6
- gate_pre: bfloat16 [1024, 16384], P('col', 'row'), may hold values from -8 to 8
- up_pre: bfloat16 [1024, 16384], P('col', 'row'), may hold values from -6 to 6
- gate_weight: bfloat16 [8192, 16384], P('col', 'row'), may hold values from -0.0625 to 0.0625
- up_weight: bfloat16 [8192, 16384], P('col', 'row'), may hold values from -0.0625 to 0.0625
- down_weight: bfloat16 [16384, 8192], P('row', 'col'), may hold values from -0.046875 to 0.046875
Outputs:
- input_grad: bfloat16 [1024, 8192], P('row', 'col')
- gate_grad: bfloat16 [8192, 16384], P('col', 'row')
- up_grad: bfloat16 [8192, 16384], P('col', 'row')
- down_grad: bfloat16 [16384, 8192], P('row', 'col')
The draws below stay inside these ranges and needn't reach their ends.
All inputs are finite; a program needn't handle non-finite values.
Results may differ from the reference program's by a relative error of at most 0.0049.
Values may be sent and summed in bfloat16 or wider, within the bound.
A program may use at most 64 MiB of HBM per device.

```python
import math
import jax
import jax.numpy as jnp

D = 8192
FF = 16384
TOKENS = 1024


def raised(result, key, source, target, shards_of, factor):
    def block_of(axis_at):
        return (jnp.arange(result.shape[axis_at]) // (result.shape[axis_at] // shards_of)).reshape((-1,) + (1,) * (result.ndim - 1 - axis_at))

    near = jax.random.permutation(key, shards_of)[block_of(target)]
    far = (block_of(target) + shards_of // 2) % shards_of
    return jnp.where((block_of(source) == near) | (block_of(source) == far), factor * result, result)


def block_scale(rng, extent, shards, smallest, high):
    factor_of, own = 1.0, jax.random.fold_in(rng, 6)
    for dim, shards_of in shards:
        heights = jnp.exp(jax.random.uniform(jax.random.fold_in(own, dim), (shards_of,), jnp.float32, smallest / len(shards), high / len(shards)))
        factor_of = factor_of * jnp.repeat(heights, extent[dim] // shards_of).reshape([-1 if axis == dim else 1 for axis in range(len(extent))])
    return factor_of


def centred(stream_key, extent, width, bound, split=(), dtype=jnp.bfloat16):
    factor_of = block_scale(stream_key, extent, split, -0.22, 0.18) if split else 1.0
    result = jax.random.normal(stream_key, extent, jnp.float32) * width * factor_of
    return jnp.minimum(jnp.maximum(result, -bound), bound).astype(dtype)


def bell_draw_with(key, extent, spread, limit, split, heavy, dtype=jnp.bfloat16):
    entries = spread * jax.random.normal(key, extent, jnp.float32)
    if split:
        entries = entries * block_scale(key, extent, split, -0.22, 0.18)
    return jnp.clip(raised(entries, jax.random.fold_in(key, 3), *heavy), -limit, limit).astype(dtype)


def setup_inputs(seed: int = 0) -> dict:
    seeds = jax.random.split(jax.random.key(seed), 8)
    inputs = centred(seeds[0], (TOKENS, D), 1.0, 6.0, ((0, 32), (1, 16)))
    grad_out = bell_draw_with(seeds[1], (TOKENS, D), 1.0, 6.0, ((0, 32), (1, 16)), (1, 0, 32, 2.75))
    gate_pre = centred(seeds[2], (TOKENS, FF), 1.5, 8.0, ((0, 16), (1, 32)))
    up_pre = centred(seeds[3], (TOKENS, FF), 1.0, 6.0, ((0, 16), (1, 32)))
    gate_weight = centred(seeds[4], (D, FF), D ** -0.5, 0.0625, ((0, 16), (1, 32)))
    up_weight = centred(seeds[5], (D, FF), D ** -0.5, 0.0625, ((0, 16), (1, 32)))
    down_weight = centred(seeds[6], (FF, D), FF ** -0.5, 0.046875, ((0, 32), (1, 16)))
    return {"inputs": inputs, "grad_out": grad_out, "gate_pre": gate_pre, "up_pre": up_pre, "gate_weight": gate_weight, "up_weight": up_weight, "down_weight": down_weight}


def reference(inputs, grad_out, gate_pre, up_pre, gate_weight, up_weight, down_weight):
    hidden_grad = jnp.dot(grad_out, down_weight.T, preferred_element_type=jnp.float32)
    gate_val = gate_pre.astype(jnp.float32)
    up_val = up_pre.astype(jnp.float32)
    sigmoid_val = jax.nn.sigmoid(gate_val)
    silu_val = gate_val * sigmoid_val
    hidden = (silu_val * up_val).astype(jnp.bfloat16)
    up_term = (hidden_grad * silu_val).astype(jnp.bfloat16)
    gate_term = (hidden_grad * up_val * sigmoid_val * (1.0 + gate_val * (1.0 - sigmoid_val))).astype(jnp.bfloat16)
    grad_scale = 1.0 / math.sqrt(TOKENS)
    down_grad = (jnp.dot(hidden.T, grad_out, preferred_element_type=jnp.float32) * grad_scale).astype(jnp.bfloat16)
    gate_grad = (jnp.dot(inputs.T, gate_term, preferred_element_type=jnp.float32) * grad_scale).astype(jnp.bfloat16)
    up_grad = (jnp.dot(inputs.T, up_term, preferred_element_type=jnp.float32) * grad_scale).astype(jnp.bfloat16)
    input_grad = (jnp.dot(gate_term, gate_weight.T, preferred_element_type=jnp.float32) + jnp.dot(up_term, up_weight.T, preferred_element_type=jnp.float32)).astype(jnp.bfloat16)
    return (input_grad, gate_grad, up_grad, down_grad)
```

```python
import functools
import math

import jax
import jax.numpy as jnp
from jax import lax
from jax.experimental import pallas as pl
from jax.experimental.pallas import tpu as pltpu
from jax.sharding import PartitionSpec as P

MESH = pl.DeviceIdType.MESH
F32 = jnp.float32
BF16 = jnp.bfloat16


def mod8(v):
    return lax.rem(v + 16, 8)


def kernel(
    scale, inp, gout, gpre, upre, gw, uw, dw,
    o_ig, o_gg, o_ug, o_dg,
    G, X, PRE, A, B, HID, dwt, gwt, uwt, PH, rs_s, rs_r, rl_s, rl_r, xs, xr, S,
    HG, TG, TU, IG, IGR, ES, ER, ACC, fs, fr, ss, rs,
):
    col = lax.axis_index("col")
    row = lax.axis_index("row")
    z, xl = lax.div(col, 2), lax.rem(col, 2)
    y, xh, co = lax.div(row, 4), lax.rem(lax.div(row, 2), 2), lax.rem(row, 2)

    def at_z(zz):
        return {"col": zz * 2 + xl, "row": row}

    def at_y(yy):
        return {"col": col, "row": yy * 4 + xh * 2 + co}

    zdev = {1: at_z(mod8(z + 1)), -1: at_z(mod8(z - 1))}
    xlo = {"col": z * 2 + 1 - xl, "row": row}
    xhi = {"col": col, "row": y * 4 + (1 - xh) * 2 + co}
    sib = {"col": col, "row": y * 4 + xh * 2 + 1 - co}
    ypeer = {d: at_y(mod8(y + d)) for d in range(1, 8)}

    names = {}
    sends = []

    def sem(name):
        return names.setdefault(name, len(names))

    def send(name, src, dst, dev):
        i = sem(name)
        c = pltpu.make_async_remote_copy(
            src_ref=src, dst_ref=dst, send_sem=ss.at[i], recv_sem=rs.at[i],
            device_id=dev, device_id_type=MESH,
        )
        c.start()
        sends.append(c)

    def recv(name, dst):
        i = sem(name)
        pltpu.make_async_remote_copy(
            src_ref=dst, dst_ref=dst, send_sem=ss.at[i], recv_sem=rs.at[i],
            device_id=sib, device_id_type=MESH,
        ).wait_recv()

    bar = pltpu.get_barrier_semaphore()
    partners = [zdev[1], zdev[-1], xlo, xhi, sib] + [ypeer[d] for d in range(1, 8)]
    for dev in partners:
        pl.semaphore_signal(bar, inc=1, device_id=dev, device_id_type=MESH)
    G[y, xh, co] = gout[...]
    X[y, xh, co] = inp[...]
    PRE[0, z, xl] = gpre[...]
    PRE[1, z, xl] = upre[...]
    dwt[...] = dw[...].T
    gwt[...] = gw[...].T
    uwt[...] = uw[...].T
    pl.semaphore_wait(bar, len(partners))

    yorder = [4, 3, 5, 2, 6, 1, 7]
    own = G.at[y, xh, co]
    for d in yorder:
        send(f"gy{d}", own, own, ypeer[d])
    send("gx0", own, own, xhi)

    def pre_send(s, k):
        blk = PRE.at[:, mod8(z - s * (k - 1)), xl]
        send(f"pz{s}{k}", blk, blk, zdev[s])

    def pre_x(tag, zz):
        blk = PRE.at[:, zz, xl]
        send(f"px{tag}", blk, blk, xlo)

    def pre_recv(s, k):
        recv(f"pz{s}{k}", PRE.at[:, mod8(z - s * k), xl])

    pre_send(1, 1)
    pre_send(-1, 1)
    pre_x("0", z)

    def gy_fwd(d):
        blk = G.at[mod8(y - d), xh, co]
        recv(f"gy{d}", blk)
        send(f"gx{d}", blk, blk, xhi)

    def pre_hop(k):
        for s in (1, -1):
            if s == 1 or k < 4:
                pre_recv(s, k)
                if k < (4 if s == 1 else 3):
                    pre_send(s, k + 1)
                pre_x(f"{s}{k}", mod8(z - s * k))

    gy_fwd(1)
    gy_fwd(7)
    gy_fwd(2)
    gy_fwd(6)
    pre_hop(1)
    gy_fwd(3)
    gy_fwd(5)
    gy_fwd(4)
    send("gs0", G.at[:, xh, co], G.at[:, xh, co], sib)
    pre_hop(2)
    for d in [0, 1, 7, 2, 6, 3, 5, 4]:
        recv(f"gx{d}", G.at[mod8(y - d), 1 - xh, co])
    send("gs1", G.at[:, 1 - xh, co], G.at[:, 1 - xh, co], sib)
    xown = X.at[y, xh, co]
    recv("gs0", G.at[:, xh, 1 - co])
    recv("gs1", G.at[:, 1 - xh, 1 - co])

    def partial(t):
        g = G[t].reshape(128, 512)
        PH[t] = jnp.dot(g, dwt[...], preferred_element_type=F32)

    streams = [(0, 1), (0, -1), (1, 1), (1, -1)]

    def hops(h, s):
        return 4 if (h == 0) == (s == 1) else 3

    def half(h):
        return pl.ds(h * 256, 256)

    def rs_step(h, s, k):
        n = hops(h, s)
        i = streams.index((h, s))
        t = mod8(z + s * (n - k + 1))
        val = PH[t, :, half(h)]
        if k > 1:
            recv(f"r{i}{k - 1}", rs_r.at[i, k - 1])
            val = val + rs_r[i, k - 1].astype(F32)
        if k == n:
            rl_s[i] = val
            send(f"r{i}{k}", rl_s.at[i], rl_r.at[i], zdev[s])
        else:
            rs_s[i, k] = val.astype(BF16)
            send(f"r{i}{k}", rs_s.at[i, k], rs_r.at[i, k], zdev[s])

    def terms(t):
        for h in (0, 1):
            g = PRE[0, t, :, :, half(h)].reshape(128, 256).astype(F32)
            u = PRE[1, t, :, :, half(h)].reshape(128, 256).astype(F32)
            sg = 1.0 / (1.0 + jnp.exp(-g))
            silu = g * sg
            A[t, :, half(h)] = silu
            HID[t, :, half(h)] = (silu * u).astype(BF16)
            B[t, :, half(h)] = u * sg * (1.0 + g * (1.0 - sg))

    def got_x(tag, zz):
        recv(f"px{tag}", PRE.at[:, zz, 1 - xl])

    partial(mod8(z + 4))
    rs_step(0, 1, 1)
    rs_step(1, -1, 1)
    partial(mod8(z + 3))
    partial(mod8(z - 3))
    rs_step(0, -1, 1)
    rs_step(1, 1, 1)
    for d in yorder:
        send(f"xy{d}", xown, xown, ypeer[d])
    for d in (2, -2, 1, -1, 0):
        partial(mod8(z + d))
    pre_hop(3)
    for i, (h, s) in enumerate(streams):
        if hops(h, s) == 4:
            rs_step(h, s, 2)
    for i, (h, s) in enumerate(streams):
        if hops(h, s) == 3:
            rs_step(h, s, 2)
    got_x("0", z)
    terms(z)
    got_x("11", mod8(z - 1))
    terms(mod8(z - 1))
    got_x("-11", mod8(z + 1))
    terms(mod8(z + 1))
    for want in (4, 3):
        for h, s in streams:
            if hops(h, s) == want:
                rs_step(h, s, 3)
    pre_hop(4)
    got_x("12", mod8(z - 2))
    terms(mod8(z - 2))
    got_x("-12", mod8(z + 2))
    terms(mod8(z + 2))
    for h, s in streams:
        if hops(h, s) == 4:
            rs_step(h, s, 4)
    S[...] = PH[z]
    for want in (3, 4):
        for i, (h, s) in enumerate(streams):
            n = hops(h, s)
            if n == want:
                recv(f"r{i}{n}", rl_r.at[i])
                S[:, half(h)] = S[:, half(h)] + rl_r[i]

    xs[...] = S[...].astype(BF16)
    send("xs", xs, xr, xlo)
    for tag, d in (("13", -3), ("-13", 3), ("14", 4)):
        got_x(tag, mod8(z + d))
        terms(mod8(z + d))
    recv("xs", xr)
    own_hg = (S[...] + xr[...].astype(F32)).astype(BF16)
    HG[z, 0] = own_hg[:, :256]
    HG[z, 1] = own_hg[:, 256:]

    def hg_send(h, s, k):
        blk = HG.at[mod8(z - s * (k - 1)), h]
        send(f"h{streams.index((h, s))}{k}", blk, blk, zdev[s])

    def hg_recv(h, s, k):
        recv(f"h{streams.index((h, s))}{k}", HG.at[mod8(z - s * k), h])

    for h, s in streams:
        hg_send(h, s, 1)

    def block(slot, t):
        for h in (0, 1):
            hg = HG[t, h].astype(F32)
            TG[t, :, half(h)] = (hg * B[t, :, half(h)]).astype(BF16)
            TU[t, :, half(h)] = (hg * A[t, :, half(h)]).astype(BF16)
        val = jnp.dot(TG[t], gwt[...], preferred_element_type=F32) + jnp.dot(
            TU[t], uwt[...], preferred_element_type=F32
        )
        IG[slot] = val.reshape(2, 2, 32, 512)
        send(f"c{slot}", IG.at[slot, :, 1 - co], IGR.at[slot], sib)

    def out_block(slot, t):
        recv(f"c{slot}", IGR.at[slot])
        val = IG[slot, :, co] + IGR[slot]

        @pl.when(t == y)
        def _():
            ACC[...] = val

        @pl.when(t != y)
        def _():
            ES[slot] = val.astype(BF16)
            e_copy(slot, t).start()

    def e_copy(slot, t):
        d = mod8(t - y)
        return pltpu.make_async_remote_copy(
            src_ref=ES.at[slot], dst_ref=ER.at[d], send_sem=ss.at[e0 + slot], recv_sem=rs.at[e0 + d],
            device_id=at_y(t), device_id_type=MESH,
        )

    e0 = 112
    slots = [0, -1, 1, -2, 2, -3, 3, 4]

    def grads(lhs, rhs, out):
        def body(i, carry):
            rows = pl.ds(pl.multiple_of(i * 128, 128), 128)
            a = lhs(rows)
            acc = lax.dot_general(a, rhs(), (((0,), (0,)), ((), ())), preferred_element_type=F32)
            out[rows, :] = (acc * scale).astype(BF16)
            return carry

        lax.fori_loop(0, 4, body, 0)

    block(0, z)
    for d in range(1, 8):
        recv(f"xy{d}", X.at[mod8(y - d), xh, co])
    send("xx", X.at[:, xh, co], X.at[:, xh, co], xhi)
    for k in (1, 2, 3, 4):
        for h, s in streams:
            if k <= hops(h, s):
                hg_recv(h, s, k)
                if k < hops(h, s):
                    hg_send(h, s, k + 1)
        if k < 4:
            block(2 * k - 1, mod8(z - k))
            block(2 * k, mod8(z + k))
        else:
            block(7, mod8(z + 4))
        if k == 1:
            out_block(0, z)
            grads(
                lambda rows: HID[:, :, rows].reshape(1024, 128),
                lambda: G[...].reshape(1024, 512),
                o_dg,
            )
        else:
            out_block(2 * k - 3, mod8(z - k + 1))
            out_block(2 * k - 2, mod8(z + k - 1))
        if k == 3:
            recv("xx", X.at[:, 1 - xh, co])
            send("xc", X.at[:, :, co], X.at[:, :, co], sib)
    out_block(7, mod8(z + 4))

    recv("xc", X.at[:, :, 1 - co])
    x_rows = lambda rows: X[:, :, :, :, rows].reshape(1024, 128)
    grads(x_rows, lambda: TG[...].reshape(1024, 512), o_gg)
    for d in range(1, 8):
        i = e0 + d
        pltpu.make_async_remote_copy(
            src_ref=ER.at[d], dst_ref=ER.at[d], send_sem=ss.at[i], recv_sem=rs.at[i],
            device_id=sib, device_id_type=MESH,
        ).wait_recv()
        ACC[...] = ACC[...] + ER[d].astype(F32)
    fs[...] = ACC[1 - xh]
    send("f", fs, fr, xhi)
    grads(x_rows, lambda: TU[...].reshape(1024, 512), o_ug)
    recv("f", fr)
    o_ig[...] = (ACC[xh] + fr[...]).astype(BF16)

    for c in sends:
        c.wait_send()
    for slot, d in enumerate(slots):
        t = mod8(z + d)

        @pl.when(t != y)
        def _():
            e_copy(slot, t).wait_send()

    assert len(names) <= e0


def per_device(inputs, grad_out, gate_pre, up_pre, gate_weight, up_weight, down_weight):
    scale = 1.0 / math.sqrt(grad_out.shape[0] * lax.axis_size("row"))
    vm = pltpu.VMEM
    return pl.pallas_call(
        functools.partial(kernel, scale),
        out_shape=(
            jax.ShapeDtypeStruct((32, 512), BF16),
            jax.ShapeDtypeStruct((512, 512), BF16),
            jax.ShapeDtypeStruct((512, 512), BF16),
            jax.ShapeDtypeStruct((512, 512), BF16),
        ),
        in_specs=[pl.BlockSpec(memory_space=vm)] * 7,
        out_specs=[pl.BlockSpec(memory_space=vm)] * 4,
        scratch_shapes=[
            vm((8, 2, 2, 32, 512), BF16),
            vm((8, 2, 2, 32, 512), BF16),
            vm((2, 8, 2, 64, 512), BF16),
            vm((8, 128, 512), F32),
            vm((8, 128, 512), F32),
            vm((8, 128, 512), BF16),
            vm((512, 512), BF16),
            vm((512, 512), BF16),
            vm((512, 512), BF16),
            vm((8, 128, 512), F32),
            vm((4, 4, 128, 256), BF16),
            vm((4, 4, 128, 256), BF16),
            vm((4, 128, 256), F32),
            vm((4, 128, 256), F32),
            vm((128, 512), BF16),
            vm((128, 512), BF16),
            vm((128, 512), F32),
            vm((8, 2, 128, 256), BF16),
            vm((8, 128, 512), BF16),
            vm((8, 128, 512), BF16),
            vm((8, 2, 2, 32, 512), F32),
            vm((8, 2, 32, 512), F32),
            vm((8, 2, 32, 512), BF16),
            vm((8, 2, 32, 512), BF16),
            vm((2, 32, 512), F32),
            vm((32, 512), F32),
            vm((32, 512), F32),
            pltpu.SemaphoreType.DMA((120,)),
            pltpu.SemaphoreType.DMA((120,)),
        ],
        compiler_params=pltpu.CompilerParams(
            collective_id=0, has_side_effects=True, vmem_limit_bytes=56 * 1024 * 1024
        ),
        name="swiglu_backward",
    )(inputs, grad_out, gate_pre, up_pre, gate_weight, up_weight, down_weight)


def solution(mesh):
    return jax.shard_map(
        per_device,
        mesh=mesh,
        in_specs=(
            P("row", "col"),
            P("row", "col"),
            P("col", "row"),
            P("col", "row"),
            P("col", "row"),
            P("col", "row"),
            P("row", "col"),
        ),
        out_specs=(P("row", "col"), P("col", "row"), P("col", "row"), P("row", "col")),
        check_vma=False,
    )
```

```python
import functools
import math

import jax
import jax.numpy as jnp
from jax import lax
from jax.experimental import pallas as pl
from jax.experimental.pallas import tpu as pltpu
from jax.sharding import PartitionSpec as P

MESH = pl.DeviceIdType.MESH
F32 = jnp.float32
BF16 = jnp.bfloat16
SEMS = 124


def mod8(v):
    return lax.rem(v + 16, 8)


def kernel(
    scale, inp, gout, gpre, upre, gw, uw, dw,
    o_ig, o_gg, o_ug, o_dg,
    G, X, PRE, A, B, HID, dwt, gwt, uwt, PH, rs_s, rs_r, rl_s, rl_r, xs, xr, S,
    HG, TG, TU, IG, IGR, ES, ER, ACC, vig, vgg, vug, vdg, vgw, vuw, vdw, ss, rs, ls,
):
    col = lax.axis_index("col")
    row = lax.axis_index("row")
    z, xl = lax.div(col, 2), lax.rem(col, 2)
    y, xh, co = lax.div(row, 4), lax.rem(lax.div(row, 2), 2), lax.rem(row, 2)

    def at_z(zz):
        return {"col": zz * 2 + xl, "row": row}

    def at_y(yy, x=None):
        return {"col": col, "row": yy * 4 + (xh if x is None else x) * 2 + co}

    zdev = {1: at_z(mod8(z + 1)), -1: at_z(mod8(z - 1))}
    xlo = {"col": z * 2 + 1 - xl, "row": row}
    xhi = at_y(y, 1 - xh)
    sib = {"col": col, "row": y * 4 + xh * 2 + 1 - co}

    names = {}

    def sem(name):
        return names.setdefault(name, len(names))

    def copy(src, dst, i, j, dev):
        return pltpu.make_async_remote_copy(
            src_ref=src, dst_ref=dst, send_sem=ss.at[i], recv_sem=rs.at[j],
            device_id=dev, device_id_type=MESH,
        )

    groups = {"g": 0, "x": 0, "p": 1, "s": 1, "v": 2, "w": 3, "e": 4, "h": 5, "r": 6, "l": 7, "c": 8}

    def send(name, src, dst, dev):
        copy(src, dst, groups[name[0]], sem(name), dev).start()

    def sent(group, ref):
        i = groups[group]
        copy(ref, ref, i, 0, sib).wait_send()

    def recv_at(i, dst):
        copy(dst, dst, i, i, sib).wait_recv()

    def recv(name, dst):
        recv_at(sem(name), dst)

    bar = pltpu.get_barrier_semaphore()
    partners = [zdev[1], zdev[-1], xlo, xhi, sib]
    partners += [at_y(mod8(y + d)) for d in range(1, 8)]
    partners += [at_y(mod8(y + d), 1 - xh) for d in range(1, 8)]
    for dev in partners:
        pl.semaphore_signal(bar, inc=1, device_id=dev, device_id_type=MESH)
    loads = [
        pltpu.make_async_copy(a, b, ls.at[4 + i])
        for i, (a, b) in enumerate(
            (
                (gout, G.at[y, xh, co]),
                (gpre, PRE.at[0, z, xl]),
                (upre, PRE.at[1, z, xl]),
                (inp, X.at[y, xh, co]),
                (dw, vdw),
                (gw, vgw),
                (uw, vuw),
            )
        )
    ]
    for c in loads:
        c.start()
    for c in loads[:4]:
        c.wait()
    pl.semaphore_wait(bar, len(partners))

    yorder = [4, 3, 5, 2, 6, 1, 7]
    need = [4, 3, -3, 2, -2, 1, -1, 0]
    own = G.at[y, xh, co]
    g0 = [sem(f"gy{d}") for d in range(8)][0]
    for d in yorder:
        send(f"gy{d}", own, own, at_y(mod8(y + d)))

    def pre_hops(a, s):
        return 4 if (a == 0) == (s == 1) else 3

    def pre_send(a, s, k):
        blk = PRE.at[a, mod8(z - s * (k - 1)), xl]
        send(f"pz{a}{s}{k}", blk, blk, zdev[s])

    def pre_x(d):
        blk = PRE.at[:, mod8(z + d), xl]
        send(f"px{d}", blk, blk, xlo)

    def pre_hop(k):
        for a in (0, 1):
            for s in (1, -1):
                n = pre_hops(a, s)
                if k <= n:
                    recv(f"pz{a}{s}{k}", PRE.at[a, mod8(z - s * k), xl])
                if k < n:
                    pre_send(a, s, k + 1)

    for a in (0, 1):
        for s in (1, -1):
            pre_send(a, s, 1)

    def g_row(j):
        t = mod8(z + j)
        d = mod8(y - t)

        @pl.when(d != 0)
        def _():
            recv_at(g0 + d, G.at[t, xh, co])

        blk = G.at[t, xh, co]
        send(f"gx{j}", blk, blk, xhi)

    def g_sib(j):
        t = mod8(z + j)
        recv(f"gx{j}", G.at[t, 1 - xh, co])
        blk = G.at[t, :, co]
        send(f"gs{j}", blk, blk, sib)

    def partial(j):
        t = mod8(z + j)
        recv(f"gs{j}", G.at[t, :, 1 - co])
        PH[t] = jnp.dot(G[t].reshape(128, 512), dwt[...], preferred_element_type=F32)

    xown = X.at[y, xh, co]
    send("xx", xown, xown, xhi)
    pre_x(0)
    for c, v, t in zip(loads[4:], (vdw, vgw, vuw), (dwt, gwt, uwt)):
        c.wait()
        t[...] = v[...].T
    g_row(4)
    pre_hop(1)
    for j in need[1:]:
        g_row(j)
    pre_x(-1)
    pre_x(1)
    for j in need[:3]:
        g_sib(j)

    slices = [0, 1, 2, 3]

    def hops(q, s):
        return 4 if (q < 2) == (s == 1) else 3

    streams = [(q, s) for n in (4, 3) for q in slices for s in (1, -1) if hops(q, s) == n]

    def cols(q):
        return pl.ds(q * 128, 128)

    def rs_step(q, s, k):
        n = hops(q, s)
        i = streams.index((q, s))
        t = mod8(z + s * (n - k + 1))
        val = PH[t, :, cols(q)]
        if k > 1:
            recv(f"r{i}{k - 1}", rs_r.at[i, k - 1])
            val = val + rs_r[i, k - 1].astype(F32)
        if k == n:
            rl_s[i] = val
            send(f"l{i}", rl_s.at[i], rl_r.at[i], zdev[s])
        else:
            rs_s[i, k] = val.astype(BF16)
            send(f"r{i}{k}", rs_s.at[i, k], rs_r.at[i, k], zdev[s])

    def rs_all(n, k):
        for q, s in streams:
            if hops(q, s) == n:
                rs_step(q, s, k)

    def terms(j):
        t = mod8(z + j)
        recv(f"px{j}", PRE.at[:, t, 1 - xl])
        for h in (0, 1):
            c = pl.ds(h * 256, 256)
            g = PRE[0, t, :, :, c].reshape(128, 256).astype(F32)
            u = PRE[1, t, :, :, c].reshape(128, 256).astype(F32)
            sg = 1.0 / (1.0 + jnp.exp(-g))
            silu = g * sg
            A[t, :, c] = silu
            HID[t, :, c] = (silu * u).astype(BF16)
            B[t, :, c] = u * sg * (1.0 + g * (1.0 - sg))

    partial(4)
    rs_all(4, 1)
    partial(3)
    partial(-3)
    rs_all(3, 1)
    pre_hop(2)
    g_sib(2)
    g_sib(-2)
    rs_all(4, 2)
    partial(2)
    partial(-2)
    rs_all(3, 2)
    for j in (1, -1, 0):
        g_sib(j)
    pre_x(-2)
    pre_x(2)
    recv("xx", X.at[y, 1 - xh, co])
    xpair = X.at[y, :, co]
    for d in yorder:
        copy(xpair, xpair, groups["v"], sem("v"), at_y(mod8(y + d))).start()
    pre_hop(3)
    rs_all(4, 3)
    partial(1)
    partial(-1)
    rs_all(3, 3)
    terms(0)
    rs_all(4, 4)
    partial(0)
    pre_hop(4)
    for q in slices:
        val = PH[z, :, cols(q)]
        for s in (1, -1):
            n = hops(q, s)
            i = streams.index((q, s))
            recv(f"l{i}", rl_r.at[i])
            val = val + rl_r[i]
        S[q] = val
        xs[q] = val.astype(BF16)
        send(f"s{q}", xs.at[q], xr.at[q], xlo)

    def hg_send(q, s, k):
        blk = HG.at[mod8(z - s * (k - 1)), q]
        send(f"h{streams.index((q, s))}{k}", blk, blk, zdev[s])

    for q in slices:
        recv(f"s{q}", xr.at[q])
        HG[z, q] = (S[q] + xr[q].astype(F32)).astype(BF16)
        hg_send(q, 1, 1)
        hg_send(q, -1, 1)
    for d in (-3, 3, 4):
        pre_x(d)

    def block(slot, j):
        t = mod8(z + j)
        for q in slices:
            hg = HG[t, q].astype(F32)
            TG[t, :, cols(q)] = (hg * B[t, :, cols(q)]).astype(BF16)
            TU[t, :, cols(q)] = (hg * A[t, :, cols(q)]).astype(BF16)
        val = jnp.dot(TG[t], gwt[...], preferred_element_type=F32) + jnp.dot(
            TU[t], uwt[...], preferred_element_type=F32
        )
        IG[slot] = val.reshape(2, 2, 32, 512)
        send(f"c{slot}", IG.at[slot, :, 1 - co], IGR.at[slot], sib)


    def e_copy(slot, j, other):
        t = mod8(z + j)
        d = mod8(t - y)
        return copy(
            ES.at[8 * other + slot], ER.at[8 * other + d], groups["e"], sem("e"),
            at_y(t, 1 - xh if other else xh),
        )

    def out_block(slot, j):
        t = mod8(z + j)
        recv(f"c{slot}", IGR.at[slot])
        ES[8 + slot] = (IG[slot, 1 - xh, co] + IGR[slot, 1 - xh]).astype(BF16)
        e_copy(slot, j, 1).start()
        val = IG[slot, xh, co] + IGR[slot, xh]

        @pl.when(t == y)
        def _():
            ACC[...] = val

        @pl.when(t != y)
        def _():
            ES[slot] = val.astype(BF16)
            e_copy(slot, j, 0).start()

    order = [0, -1, 1, -2, 2, -3, 3, 4]

    def grads(lhs, rhs, vout, out, i):
        def body(n, carry):
            rows = pl.ds(pl.multiple_of(n * 128, 128), 128)
            acc = lax.dot_general(
                lhs(rows), rhs(), (((0,), (0,)), ((), ())), preferred_element_type=F32
            )
            vout[rows, :] = (acc * scale).astype(BF16)
            return carry

        lax.fori_loop(0, 4, body, 0)
        pltpu.make_async_copy(vout, out, ls.at[i]).start()

    block(0, 0)
    for k in (1, 2, 3, 4):
        for q, s in streams:
            if k <= hops(q, s):
                recv(f"h{streams.index((q, s))}{k}", HG.at[mod8(z - s * k), q])
                if k < hops(q, s):
                    hg_send(q, s, k + 1)
        mine = (-k, k) if k < 4 else (4,)
        for j in mine:
            terms(j)
        for j in mine:
            block(order.index(j), j)
        for j in (0,) if k == 1 else (1 - k, k - 1):
            out_block(order.index(j), j)
        if k == 3:
            recv("v", X.at[pl.ds(0, 7), 0])
            send("w", X.at[:, :, co], X.at[:, :, co], sib)
    out_block(7, 4)

    x_rows = lambda rows: X[:, :, :, :, rows].reshape(1024, 128)
    h_rows = lambda rows: HID[:, :, rows].reshape(1024, 128)
    grads(h_rows, lambda: G[...].reshape(1024, 512), vdg, o_dg, 0)
    recv("w", X.at[:, :, 1 - co])
    grads(x_rows, lambda: TG[...].reshape(1024, 512), vgg, o_gg, 1)
    grads(x_rows, lambda: TU[...].reshape(1024, 512), vug, o_ug, 2)
    recv("e", ER.at[pl.ds(1, 15)])
    total = ACC[...]
    for i in range(1, 16):
        total = total + ER[i].astype(F32)
    vig[...] = total.astype(BF16)
    pltpu.make_async_copy(vig, o_ig, ls.at[3]).start()

    sent("g", G)
    sent("p", PRE)
    sent("v", X.at[pl.ds(0, 7), 0])
    sent("w", X.at[pl.ds(0, 4)])
    sent("e", ES.at[pl.ds(0, 15)])
    sent("h", HG.at[pl.ds(0, 7)])
    sent("r", rs_s.at[pl.ds(0, 5)])
    sent("l", rl_s)
    sent("c", IGR)
    for i, (v, o) in enumerate(((vdg, o_dg), (vgg, o_gg), (vug, o_ug), (vig, o_ig))):
        pltpu.make_async_copy(v, o, ls.at[i]).wait()

    assert len(names) <= SEMS, len(names)


def hand_over(*refs):
    ins, outs, sems = refs[:4], refs[4:8], refs[8]
    copies = [pltpu.make_async_copy(a, b, sems.at[i]) for i, (a, b) in enumerate(zip(ins, outs))]
    for c in copies:
        c.start()
    for c in copies:
        c.wait()


def per_device(inputs, grad_out, gate_pre, up_pre, gate_weight, up_weight, down_weight):
    scale = 1.0 / math.sqrt(grad_out.shape[0] * lax.axis_size("row"))
    vm = pltpu.VMEM
    anywhere = pl.BlockSpec(memory_space=pl.ANY)
    shapes = (
        jax.ShapeDtypeStruct((32, 512), BF16),
        jax.ShapeDtypeStruct((512, 512), BF16),
        jax.ShapeDtypeStruct((512, 512), BF16),
        jax.ShapeDtypeStruct((512, 512), BF16),
    )
    parts = pl.pallas_call(
        functools.partial(kernel, scale),
        out_shape=shapes,
        in_specs=[anywhere] * 7,
        out_specs=[anywhere] * 4,
        scratch_shapes=[
            vm((8, 2, 2, 32, 512), BF16),
            vm((8, 2, 2, 32, 512), BF16),
            vm((2, 8, 2, 64, 512), BF16),
            vm((8, 128, 512), F32),
            vm((8, 128, 512), F32),
            vm((8, 128, 512), BF16),
            vm((512, 512), BF16),
            vm((512, 512), BF16),
            vm((512, 512), BF16),
            vm((8, 128, 512), F32),
            vm((8, 4, 128, 128), BF16),
            vm((8, 4, 128, 128), BF16),
            vm((8, 128, 128), F32),
            vm((8, 128, 128), F32),
            vm((4, 128, 128), BF16),
            vm((4, 128, 128), BF16),
            vm((4, 128, 128), F32),
            vm((8, 4, 128, 128), BF16),
            vm((8, 128, 512), BF16),
            vm((8, 128, 512), BF16),
            vm((8, 2, 2, 32, 512), F32),
            vm((8, 2, 32, 512), F32),
            vm((16, 32, 512), BF16),
            vm((16, 32, 512), BF16),
            vm((32, 512), F32),
            vm((32, 512), BF16),
            vm((512, 512), BF16),
            vm((512, 512), BF16),
            vm((512, 512), BF16),
            vm((512, 512), BF16),
            vm((512, 512), BF16),
            vm((512, 512), BF16),
            pltpu.SemaphoreType.DMA((9,)),
            pltpu.SemaphoreType.DMA((SEMS,)),
            pltpu.SemaphoreType.DMA((11,)),
        ],
        compiler_params=pltpu.CompilerParams(
            collective_id=0, has_side_effects=True, vmem_limit_bytes=56 * 1024 * 1024
        ),
        name="swiglu_backward",
    )(inputs, grad_out, gate_pre, up_pre, gate_weight, up_weight, down_weight)
    return pl.pallas_call(
        hand_over,
        out_shape=shapes,
        in_specs=[pl.BlockSpec(memory_space=vm)] * 4,
        out_specs=[anywhere] * 4,
        scratch_shapes=[pltpu.SemaphoreType.DMA((4,))],
        name="hand_over",
    )(*parts)


def solution(mesh):
    return jax.shard_map(
        per_device,
        mesh=mesh,
        in_specs=(
            P("row", "col"),
            P("row", "col"),
            P("col", "row"),
            P("col", "row"),
            P("col", "row"),
            P("col", "row"),
            P("row", "col"),
        ),
        out_specs=(P("row", "col"), P("col", "row"), P("col", "row"), P("row", "col")),
        check_vma=False,
    )
```

```python
import functools
import math

import jax
import jax.numpy as jnp
from jax import lax
from jax.experimental import pallas as pl
from jax.experimental.pallas import tpu as pltpu
from jax.sharding import PartitionSpec as P

MESH = pl.DeviceIdType.MESH
F32 = jnp.float32
BF16 = jnp.bfloat16
SEMS = 121


def mod8(v):
    return lax.rem(v + 16, 8)


def kernel(
    scale, inp, gout, gpre, upre, gw, uw, dw,
    o_ig, o_gg, o_ug, o_dg,
    G, X, PRE, A, B, HID, dwt, gwt, uwt, PH, rs_s, rs_r, rl_s, rl_r, xs, xr, S,
    HG, TG, TU, IG, IGR, ES, ER, ACC, DG, GG, UG, vgw, vuw, vdw, ss, rs, ls,
):
    col = lax.axis_index("col")
    row = lax.axis_index("row")
    z, xl = lax.div(col, 2), lax.rem(col, 2)
    y, xh, co = lax.div(row, 4), lax.rem(lax.div(row, 2), 2), lax.rem(row, 2)

    def at_z(zz):
        return {"col": zz * 2 + xl, "row": row}

    def at_y(yy, x=None):
        return {"col": col, "row": yy * 4 + (xh if x is None else x) * 2 + co}

    zdev = {1: at_z(mod8(z + 1)), -1: at_z(mod8(z - 1))}
    xlo = {"col": z * 2 + 1 - xl, "row": row}
    xhi = at_y(y, 1 - xh)
    sib = {"col": col, "row": y * 4 + xh * 2 + 1 - co}

    names = {}

    def sem(name):
        return names.setdefault(name, len(names))

    def copy(src, dst, i, j, dev):
        return pltpu.make_async_remote_copy(
            src_ref=src, dst_ref=dst, send_sem=ss.at[i], recv_sem=rs.at[j],
            device_id=dev, device_id_type=MESH,
        )

    groups = {"g": 0, "x": 0, "p": 1, "s": 1, "v": 2, "w": 3, "e": 4, "h": 5, "r": 6, "l": 7, "c": 8}

    def send(name, src, dst, dev):
        copy(src, dst, groups[name[0]], sem(name), dev).start()

    def sent(group, ref):
        i = groups[group]
        copy(ref, ref, i, 0, sib).wait_send()

    def recv_at(i, dst):
        copy(dst, dst, i, i, sib).wait_recv()

    def recv(name, dst):
        recv_at(sem(name), dst)

    bar = pltpu.get_barrier_semaphore()
    partners = [zdev[1], zdev[-1], xlo, xhi, sib]
    partners += [at_y(mod8(y + d)) for d in range(1, 8)]
    partners += [at_y(mod8(y + d), 1 - xh) for d in range(1, 8)]
    for dev in partners:
        pl.semaphore_signal(bar, inc=1, device_id=dev, device_id_type=MESH)
    loads = [
        pltpu.make_async_copy(a, b, ls.at[i])
        for i, (a, b) in enumerate(
            (
                (gout, G.at[y, xh, co]),
                (gpre, PRE.at[0, z, xl]),
                (upre, PRE.at[1, z, xl]),
                (inp, X.at[y, xh, co]),
                (dw, vdw),
                (gw, vgw),
                (uw, vuw),
            )
        )
    ]
    for c in loads:
        c.start()
    pl.semaphore_wait(bar, len(partners))
    for c in loads[:4]:
        c.wait()

    yorder = [4, 3, 5, 2, 6, 1, 7]
    need = [4, 3, -3, 2, -2, 1, -1, 0]
    own = G.at[y, xh, co]
    g0 = [sem(f"gy{d}") for d in range(8)][0]
    for d in yorder:
        send(f"gy{d}", own, own, at_y(mod8(y + d)))

    def pre_hops(a, s):
        return 4 if (a == 0) == (s == 1) else 3

    def pre_send(a, s, k):
        blk = PRE.at[a, mod8(z - s * (k - 1)), xl]
        send(f"pz{a}{s}{k}", blk, blk, zdev[s])

    def pre_x(d):
        blk = PRE.at[:, mod8(z + d), xl]
        send(f"px{d}", blk, blk, xlo)

    def pre_recv(k):
        for a in (0, 1):
            for s in (1, -1):
                if k <= pre_hops(a, s):
                    recv(f"pz{a}{s}{k}", PRE.at[a, mod8(z - s * k), xl])

    def pre_next(k):
        for a in (0, 1):
            for s in (1, -1):
                if k < pre_hops(a, s):
                    pre_send(a, s, k + 1)

    for a in (0, 1):
        for s in (1, -1):
            pre_send(a, s, 1)

    def g_row(j):
        t = mod8(z + j)
        d = mod8(y - t)

        @pl.when(d != 0)
        def _():
            recv_at(g0 + d, G.at[t, xh, co])

        blk = G.at[t, xh, co]
        send(f"gx{j}", blk, blk, xhi)

    def g_sib(j):
        t = mod8(z + j)
        recv(f"gx{j}", G.at[t, 1 - xh, co])
        blk = G.at[t, :, co]
        send(f"gs{j}", blk, blk, sib)

    def partial(j):
        t = mod8(z + j)
        recv(f"gs{j}", G.at[t, :, 1 - co])
        PH[t] = jnp.dot(G[t].reshape(128, 512), dwt[...], preferred_element_type=F32)

    xown = X.at[y, xh, co]
    send("xx", xown, xown, xhi)
    pre_x(0)
    for c, v, t in zip(loads[4:], (vdw, vgw, vuw), (dwt, gwt, uwt)):
        c.wait()
        t[...] = v[...].T
    pre_recv(1)
    pre_next(1)
    for j in need:
        g_row(j)
    pre_x(-1)
    pre_x(1)
    for j in need[:3]:
        g_sib(j)

    slices = [0, 1, 2, 3]

    def hops(q, s):
        return 4 if (q < 2) == (s == 1) else 3

    streams = [(q, s) for n in (4, 3) for q in slices for s in (1, -1) if hops(q, s) == n]

    def cols(q):
        return pl.ds(q * 128, 128)

    def rs_step(q, s, k):
        n = hops(q, s)
        i = streams.index((q, s))
        t = mod8(z + s * (n - k + 1))
        val = PH[t, :, cols(q)]
        if k > 1:
            recv(f"r{i}{k - 1}", rs_r.at[i, k - 1])
            val = val + rs_r[i, k - 1].astype(F32)
        if k == 4:
            rl_s[i] = val
            send(f"l{i}", rl_s.at[i], rl_r.at[i], zdev[s])
        else:
            rs_s[i, k] = val.astype(BF16)
            send(f"r{i}{k}", rs_s.at[i, k], rs_r.at[i, k], zdev[s])

    def rs_all(n, k):
        for q, s in streams:
            if hops(q, s) == n:
                rs_step(q, s, k)

    def terms(j):
        t = mod8(z + j)
        recv(f"px{j}", PRE.at[:, t, 1 - xl])
        for h in (0, 1):
            c = pl.ds(h * 256, 256)
            g = PRE[0, t, :, :, c].reshape(128, 256).astype(F32)
            u = PRE[1, t, :, :, c].reshape(128, 256).astype(F32)
            sg = 1.0 / (1.0 + jnp.exp(-g))
            silu = g * sg
            A[t, :, c] = silu
            HID[t, :, c] = (silu * u).astype(BF16)
            B[t, :, c] = u * sg * (1.0 + g * (1.0 - sg))

    partial(4)
    rs_all(4, 1)
    partial(3)
    partial(-3)
    rs_all(3, 1)
    g_sib(2)
    g_sib(-2)
    rs_all(4, 2)
    partial(2)
    partial(-2)
    rs_all(3, 2)
    pre_recv(2)
    for j in (1, -1, 0):
        g_sib(j)
    pre_x(-2)
    pre_x(2)
    recv("xx", X.at[y, 1 - xh, co])
    xpair = X.at[y, :, co]
    for d in yorder:
        copy(xpair, xpair, groups["v"], sem("v"), at_y(mod8(y + d))).start()
    rs_all(4, 3)
    partial(1)
    partial(-1)
    rs_all(3, 3)
    terms(0)
    rs_all(4, 4)
    partial(0)
    pre_next(2)
    terms(-1)
    terms(1)
    for q in slices:
        val = PH[z, :, cols(q)]
        for s in (1, -1):
            n = hops(q, s)
            i = streams.index((q, s))
            if n == 4:
                recv(f"l{i}", rl_r.at[i])
                val = val + rl_r[i]
            else:
                recv(f"r{i}{n}", rs_r.at[i, n])
                val = val + rs_r[i, n].astype(F32)
        S[q] = val
        xs[q] = val.astype(BF16)
        send(f"s{q}", xs.at[q], xr.at[q], xlo)

    def hg_send(q, s, k):
        blk = HG.at[mod8(z - s * (k - 1)), q]
        send(f"h{streams.index((q, s))}{k}", blk, blk, zdev[s])

    recv("v", X.at[pl.ds(0, 7), 0])
    send("w", X.at[:, :, co], X.at[:, :, co], sib)
    for q in slices:
        recv(f"s{q}", xr.at[q])
        HG[z, q] = (S[q] + xr[q].astype(F32)).astype(BF16)
        hg_send(q, 1, 1)
        hg_send(q, -1, 1)
    pre_recv(3)
    pre_next(3)
    pre_x(-3)
    pre_x(3)

    def block(slot, j):
        t = mod8(z + j)
        for q in slices:
            hg = HG[t, q].astype(F32)
            TG[t, :, cols(q)] = (hg * B[t, :, cols(q)]).astype(BF16)
            TU[t, :, cols(q)] = (hg * A[t, :, cols(q)]).astype(BF16)
        val = jnp.dot(TG[t], gwt[...], preferred_element_type=F32) + jnp.dot(
            TU[t], uwt[...], preferred_element_type=F32
        )
        IG[slot] = val.reshape(2, 2, 32, 512)
        send(f"c{slot}", IG.at[slot, :, 1 - co], IGR.at[slot], sib)


    def e_copy(slot, j, other):
        t = mod8(z + j)
        d = mod8(t - y)
        return copy(
            ES.at[8 * other + slot], ER.at[8 * other + d], groups["e"], sem("e"),
            at_y(t, 1 - xh if other else xh),
        )

    def out_block(slot, j):
        t = mod8(z + j)
        recv(f"c{slot}", IGR.at[slot])
        ES[8 + slot] = (IG[slot, 1 - xh, co] + IGR[slot, 1 - xh]).astype(BF16)
        e_copy(slot, j, 1).start()
        val = IG[slot, xh, co] + IGR[slot, xh]

        @pl.when(t == y)
        def _():
            ACC[...] = val

        @pl.when(t != y)
        def _():
            ES[slot] = val.astype(BF16)
            e_copy(slot, j, 0).start()

    order = [0, -1, 1, -2, 2, -3, 3, 4]

    def grads(*js):
        def body(n, carry):
            rows = pl.ds(pl.multiple_of(n * 256, 256), 256)
            tot = [None, None, None]
            for j in js:
                t = mod8(z + j)
                h = HID[t, :, rows]
                x = X[t, :, :, :, rows].reshape(128, 256)
                for i, (l, r) in enumerate(((h, G[t].reshape(128, 512)), (x, TG[t]), (x, TU[t]))):
                    p = lax.dot_general(l, r, (((0,), (0,)), ((), ())), preferred_element_type=F32)
                    tot[i] = p if tot[i] is None else tot[i] + p
            for i, (acc, v) in enumerate(zip((DG, GG, UG), (o_dg, o_gg, o_ug))):
                if js[0] != 0:
                    tot[i] = tot[i] + acc[rows, :]
                if js[-1] == 4:
                    v[rows, :] = (tot[i] * scale).astype(BF16)
                else:
                    acc[rows, :] = tot[i]
            return carry

        lax.fori_loop(0, 2, body, 0)

    block(0, 0)
    recv("w", X.at[:, :, 1 - co])
    grads(0)
    out_block(0, 0)
    for k in (1, 2, 3, 4):
        for q, s in streams:
            if k <= hops(q, s):
                recv(f"h{streams.index((q, s))}{k}", HG.at[mod8(z - s * k), q])
                if k < hops(q, s):
                    hg_send(q, s, k + 1)
        mine = (-k, k) if k < 4 else (4,)
        for j in mine:
            if k > 1:
                terms(j)
        if k == 2:
            pre_recv(4)
            pre_x(4)
        for j in mine:
            block(order.index(j), j)
        if k in (2, 3):
            grads(1 - k, k - 1)
        for j in mine:
            out_block(order.index(j), j)

    grads(-3, 3)
    grads(4)
    recv("e", ER.at[pl.ds(1, 15)])
    total = ACC[...]
    for i in range(1, 16):
        total = total + ER[i].astype(F32)
    o_ig[...] = total.astype(BF16)

    sent("g", G)
    sent("p", PRE)
    sent("v", X.at[pl.ds(0, 7), 0])
    sent("w", X.at[pl.ds(0, 4)])
    sent("e", ES.at[pl.ds(0, 15)])
    sent("h", HG.at[pl.ds(0, 7)])
    sent("r", rs_s.at[pl.ds(0, 6)])
    sent("l", rl_s)
    sent("c", IGR)
    assert len(names) <= SEMS, len(names)


def hand_over(*refs):
    ins, outs, sems = refs[:4], refs[4:8], refs[8]
    copies = [pltpu.make_async_copy(a, b, sems.at[i]) for i, (a, b) in enumerate(zip(ins, outs))]
    for c in copies:
        c.start()
    for c in copies:
        c.wait()


def per_device(inputs, grad_out, gate_pre, up_pre, gate_weight, up_weight, down_weight):
    scale = 1.0 / math.sqrt(grad_out.shape[0] * lax.axis_size("row"))
    vm = pltpu.VMEM
    anywhere = pl.BlockSpec(memory_space=pl.ANY)
    shapes = (
        jax.ShapeDtypeStruct((32, 512), BF16),
        jax.ShapeDtypeStruct((512, 512), BF16),
        jax.ShapeDtypeStruct((512, 512), BF16),
        jax.ShapeDtypeStruct((512, 512), BF16),
    )
    parts = pl.pallas_call(
        functools.partial(kernel, scale),
        out_shape=tuple(vm(a.shape, a.dtype) for a in shapes),
        in_specs=[anywhere] * 7,
        out_specs=[pl.BlockSpec(memory_space=vm)] * 4,
        scratch_shapes=[
            vm((8, 2, 2, 32, 512), BF16),
            vm((8, 2, 2, 32, 512), BF16),
            vm((2, 8, 2, 64, 512), BF16),
            vm((8, 128, 512), F32),
            vm((8, 128, 512), F32),
            vm((8, 128, 512), BF16),
            vm((512, 512), BF16),
            vm((512, 512), BF16),
            vm((512, 512), BF16),
            vm((8, 128, 512), F32),
            vm((8, 4, 128, 128), BF16),
            vm((8, 4, 128, 128), BF16),
            vm((4, 128, 128), F32),
            vm((4, 128, 128), F32),
            vm((4, 128, 128), BF16),
            vm((4, 128, 128), BF16),
            vm((4, 128, 128), F32),
            vm((8, 4, 128, 128), BF16),
            vm((8, 128, 512), BF16),
            vm((8, 128, 512), BF16),
            vm((8, 2, 2, 32, 512), F32),
            vm((8, 2, 32, 512), F32),
            vm((16, 32, 512), BF16),
            vm((16, 32, 512), BF16),
            vm((32, 512), F32),
            vm((512, 512), F32),
            vm((512, 512), F32),
            vm((512, 512), F32),
            vm((512, 512), BF16),
            vm((512, 512), BF16),
            vm((512, 512), BF16),
            pltpu.SemaphoreType.DMA((9,)),
            pltpu.SemaphoreType.DMA((SEMS,)),
            pltpu.SemaphoreType.DMA((7,)),
        ],
        compiler_params=pltpu.CompilerParams(
            collective_id=0, has_side_effects=True, vmem_limit_bytes=56 * 1024 * 1024
        ),
        name="swiglu_backward",
    )(inputs, grad_out, gate_pre, up_pre, gate_weight, up_weight, down_weight)
    return pl.pallas_call(
        hand_over,
        out_shape=shapes,
        in_specs=[pl.BlockSpec(memory_space=vm)] * 4,
        out_specs=[anywhere] * 4,
        scratch_shapes=[pltpu.SemaphoreType.DMA((4,))],
        name="hand_over",
    )(*[pltpu.with_memory_space_constraint(p, pltpu.VMEM) for p in parts])


def solution(mesh):
    return jax.shard_map(
        per_device,
        mesh=mesh,
        in_specs=(
            P("row", "col"),
            P("row", "col"),
            P("col", "row"),
            P("col", "row"),
            P("col", "row"),
            P("col", "row"),
            P("row", "col"),
        ),
        out_specs=(P("row", "col"), P("col", "row"), P("col", "row"), P("row", "col")),
        check_vma=False,
    )
```

```python
import functools
import math

import jax
import jax.numpy as jnp
from jax import lax
from jax.experimental import pallas as pl
from jax.experimental.pallas import tpu as pltpu
from jax.sharding import PartitionSpec as P

MESH = pl.DeviceIdType.MESH
F32 = jnp.float32
BF16 = jnp.bfloat16
SEMS = 121


def mod8(v):
    return lax.rem(v + 16, 8)


def kernel(
    scale, inp, gout, gpre, upre, gw, uw, dw,
    o_ig, o_gg, o_ug, o_dg,
    G, X, PRE, A, B, HT, XT, dwt, gwt, uwt, PH, rs_s, rs_r, rl_s, rl_r, xs, xr, S,
    HG, TG, TU, IG, IGR, ES, ER, ACC, vgw, vuw, vdw, ss, rs, ls,
):
    col = lax.axis_index("col")
    row = lax.axis_index("row")
    z, xl = lax.div(col, 2), lax.rem(col, 2)
    y, xh, co = lax.div(row, 4), lax.rem(lax.div(row, 2), 2), lax.rem(row, 2)

    def at_z(zz):
        return {"col": zz * 2 + xl, "row": row}

    def at_y(yy, x=None):
        return {"col": col, "row": yy * 4 + (xh if x is None else x) * 2 + co}

    zdev = {1: at_z(mod8(z + 1)), -1: at_z(mod8(z - 1))}
    xlo = {"col": z * 2 + 1 - xl, "row": row}
    xhi = at_y(y, 1 - xh)
    sib = {"col": col, "row": y * 4 + xh * 2 + 1 - co}

    names = {}

    def sem(name):
        return names.setdefault(name, len(names))

    def copy(src, dst, i, j, dev):
        return pltpu.make_async_remote_copy(
            src_ref=src, dst_ref=dst, send_sem=ss.at[i], recv_sem=rs.at[j],
            device_id=dev, device_id_type=MESH,
        )

    groups = {"g": 0, "x": 0, "p": 1, "s": 1, "v": 2, "w": 3, "e": 4, "h": 5, "r": 6, "l": 7, "c": 8}

    def send(name, src, dst, dev):
        copy(src, dst, groups[name[0]], sem(name), dev).start()

    def sent(group, ref):
        i = groups[group]
        copy(ref, ref, i, 0, sib).wait_send()

    def recv_at(i, dst):
        copy(dst, dst, i, i, sib).wait_recv()

    def recv(name, dst):
        recv_at(sem(name), dst)

    bar = pltpu.get_barrier_semaphore()
    partners = [zdev[1], zdev[-1], xlo, xhi, sib]
    partners += [at_y(mod8(y + d)) for d in range(1, 8)]
    partners += [at_y(mod8(y + d), 1 - xh) for d in range(1, 8)]
    for dev in partners:
        pl.semaphore_signal(bar, inc=1, device_id=dev, device_id_type=MESH)
    loads = [
        pltpu.make_async_copy(a, b, ls.at[i])
        for i, (a, b) in enumerate(
            (
                (gout, G.at[y, xh, co]),
                (gpre, PRE.at[0, z, xl]),
                (upre, PRE.at[1, z, xl]),
                (inp, X.at[y, xh, co]),
                (dw, vdw),
                (gw, vgw),
                (uw, vuw),
            )
        )
    ]
    for c in loads:
        c.start()
    pl.semaphore_wait(bar, len(partners))
    for c in loads[:4]:
        c.wait()

    yorder = [4, 3, 5, 2, 6, 1, 7]
    need = [4, 3, -3, 2, -2, 1, -1, 0]
    own = G.at[y, xh, co]
    g0 = [sem(f"gy{d}") for d in range(8)][0]
    for d in yorder:
        send(f"gy{d}", own, own, at_y(mod8(y + d)))

    def pre_hops(a, s):
        return 4 if (a == 0) == (s == 1) else 3

    def pre_send(a, s, k):
        blk = PRE.at[a, mod8(z - s * (k - 1)), xl]
        send(f"pz{a}{s}{k}", blk, blk, zdev[s])

    def pre_x(d):
        blk = PRE.at[:, mod8(z + d), xl]
        send(f"px{d}", blk, blk, xlo)

    def pre_hop(k, get=True, put=True):
        for a in (0, 1):
            for s in (1, -1):
                if get and k <= pre_hops(a, s):
                    recv(f"pz{a}{s}{k}", PRE.at[a, mod8(z - s * k), xl])
                if put and k < pre_hops(a, s):
                    pre_send(a, s, k + 1)

    for a in (0, 1):
        for s in (1, -1):
            pre_send(a, s, 1)

    def g_row(j):
        t = mod8(z + j)
        d = mod8(y - t)

        @pl.when(d != 0)
        def _():
            recv_at(g0 + d, G.at[t, xh, co])

        blk = G.at[t, xh, co]
        send(f"gx{j}", blk, blk, xhi)

    def g_sib(j):
        t = mod8(z + j)
        recv(f"gx{j}", G.at[t, 1 - xh, co])
        blk = G.at[t, :, co]
        send(f"gs{j}", blk, blk, sib)

    def partial(j):
        t = mod8(z + j)
        recv(f"gs{j}", G.at[t, :, 1 - co])
        PH[t] = jnp.dot(G[t].reshape(128, 512), dwt[...], preferred_element_type=F32)

    xown = X.at[y, xh, co]
    send("xx", xown, xown, xhi)
    pre_x(0)
    for c, v, t in zip(loads[4:], (vdw, vgw, vuw), (dwt, gwt, uwt)):
        c.wait()
        t[...] = v[...].T
    pre_hop(1)
    other = PRE.at[:, z, 1 - xl]
    recv("px0", other)
    for s in (1, -1):
        send(f"py{s}", other, other, zdev[s])
    for j in need:
        g_row(j)
    pre_hop(2)
    for j in need[:3]:
        g_sib(j)

    slices = [0, 1, 2, 3]

    def hops(q, s):
        return 4 if (q < 2) == (s == 1) else 3

    mixed = [0, 2, 1, 3]
    streams = [(q, s) for n in (4, 3) for q in mixed for s in (1, -1) if hops(q, s) == n]

    def cols(q):
        return pl.ds(q * 128, 128)

    def rs_step(q, s, k):
        n = hops(q, s)
        i = streams.index((q, s))
        t = mod8(z + s * (n - k + 1))
        val = PH[t, :, cols(q)]
        if k > 1:
            recv(f"r{i}{k - 1}", rs_r.at[i, k - 1])
            val = val + rs_r[i, k - 1].astype(F32)
        if k == 4:
            rl_s[i] = val
            send(f"l{i}", rl_s.at[i], rl_r.at[i], zdev[s])
        else:
            rs_s[i, k] = val.astype(BF16)
            send(f"r{i}{k}", rs_s.at[i, k], rs_r.at[i, k], zdev[s])

    def rs_all(n, k):
        for q, s in streams:
            if hops(q, s) == n:
                rs_step(q, s, k)

    def tokens(t):
        return pl.ds(pl.multiple_of(t * 128, 128), 128)

    def terms(j):
        t = mod8(z + j)
        if j:
            recv(f"py{-j}" if j in (1, -1) else f"px{j}", PRE.at[:, t, 1 - xl])
        for h in (0, 1):
            c = pl.ds(h * 256, 256)
            g = PRE[0, t, :, :, c].reshape(128, 256).astype(F32)
            u = PRE[1, t, :, :, c].reshape(128, 256).astype(F32)
            sg = 1.0 / (1.0 + jnp.exp(-g))
            silu = g * sg
            A[t, :, c] = silu
            HT[c, tokens(t)] = (silu * u).astype(BF16).T
            B[t, :, c] = u * sg * (1.0 + g * (1.0 - sg))

    partial(4)
    rs_all(4, 1)
    partial(3)
    partial(-3)
    rs_all(3, 1)
    pre_x(-2)
    pre_x(2)
    g_sib(2)
    g_sib(-2)
    rs_all(4, 2)
    partial(2)
    partial(-2)
    rs_all(3, 2)
    for j in (1, -1, 0):
        g_sib(j)
    recv("xx", X.at[y, 1 - xh, co])
    xpair = X.at[y, :, co]
    for d in yorder:
        copy(xpair, xpair, groups["v"], sem("v"), at_y(mod8(y + d))).start()
    rs_all(4, 3)
    partial(1)
    partial(-1)
    pre_hop(3, put=False)
    pre_x(-3)
    pre_x(3)
    rs_all(3, 3)
    terms(0)
    rs_all(4, 4)
    partial(0)
    pre_hop(3, get=False)
    terms(-1)
    terms(1)
    for q in mixed:
        val = PH[z, :, cols(q)]
        for s in (1, -1):
            n = hops(q, s)
            i = streams.index((q, s))
            if n == 4:
                recv(f"l{i}", rl_r.at[i])
                val = val + rl_r[i]
            else:
                recv(f"r{i}{n}", rs_r.at[i, n])
                val = val + rs_r[i, n].astype(F32)
        S[q] = val
        xs[q] = val.astype(BF16)
        send(f"s{q}", xs.at[q], xr.at[q], xlo)

    def hg_send(q, s, k):
        blk = HG.at[mod8(z - s * (k - 1)), q]
        send(f"h{streams.index((q, s))}{k}", blk, blk, zdev[s])

    for q in mixed:
        recv(f"s{q}", xr.at[q])
        HG[z, q] = (S[q] + xr[q].astype(F32)).astype(BF16)
        hg_send(q, 1, 1)
        hg_send(q, -1, 1)

    def block(slot, j):
        t = mod8(z + j)
        for q in slices:
            hg = HG[t, q].astype(F32)
            TG[t, :, cols(q)] = (hg * B[t, :, cols(q)]).astype(BF16)
            TU[t, :, cols(q)] = (hg * A[t, :, cols(q)]).astype(BF16)
        val = jnp.dot(TG[t], gwt[...], preferred_element_type=F32) + jnp.dot(
            TU[t], uwt[...], preferred_element_type=F32
        )
        IG[slot] = val.reshape(2, 2, 32, 512)
        send(f"c{slot}", IG.at[slot, :, 1 - co], IGR.at[slot], sib)


    def e_copy(slot, j, other):
        t = mod8(z + j)
        d = mod8(t - y)
        return copy(
            ES.at[8 * other + slot], ER.at[8 * other + d], groups["e"], sem("e"),
            at_y(t, 1 - xh if other else xh),
        )

    def out_block(slot, j):
        t = mod8(z + j)
        recv(f"c{slot}", IGR.at[slot])
        ES[8 + slot] = (IG[slot, 1 - xh, co] + IGR[slot, 1 - xh]).astype(BF16)
        e_copy(slot, j, 1).start()
        val = IG[slot, xh, co] + IGR[slot, xh]

        @pl.when(t == y)
        def _():
            ACC[...] = val

        @pl.when(t != y)
        def _():
            ES[slot] = val.astype(BF16)
            e_copy(slot, j, 0).start()

    order = [0, -1, 1, -2, 2, -3, 3, 4]

    def grad(lhs, rhs, out):
        def body(n, carry):
            rows = pl.ds(pl.multiple_of(n * 256, 256), 256)
            acc = jnp.dot(lhs[rows, :], rhs[...].reshape(1024, 512), preferred_element_type=F32)
            out[rows, :] = (acc * scale).astype(BF16)
            return carry

        lax.fori_loop(0, 2, body, 0)

    def hop(n, k):
        for q, s in streams:
            if hops(q, s) == n:
                recv(f"h{streams.index((q, s))}{k}", HG.at[mod8(z - s * k), q])
                if k < n:
                    hg_send(q, s, k + 1)

    def blocks(*js):
        for j in js:
            block(order.index(j), j)

    def outs(*js):
        for j in js:
            out_block(order.index(j), j)

    blocks(0)
    hop(4, 1)
    terms(-2)
    terms(2)
    outs(0)
    hop(3, 1)
    pre_hop(4)
    pre_x(4)
    blocks(-1, 1)
    recv("v", X.at[pl.ds(0, 7), 0])
    send("w", X.at[:, :, co], X.at[:, :, co], sib)
    hop(4, 2)
    outs(-1, 1)
    hop(3, 2)
    blocks(-2, 2)
    recv("w", X.at[:, :, 1 - co])
    for t in range(8):
        XT[:, t * 128 : t * 128 + 128] = X[t].reshape(128, 512).T
    hop(4, 3)
    outs(-2, 2)
    hop(3, 3)
    terms(-3)
    terms(3)
    blocks(-3, 3)
    terms(4)
    outs(-3, 3)
    hop(4, 4)
    blocks(4)
    outs(4)

    grad(HT, G, o_dg)
    grad(XT, TG, o_gg)
    grad(XT, TU, o_ug)
    recv("e", ER.at[pl.ds(1, 15)])
    total = ACC[...]
    for i in range(1, 16):
        total = total + ER[i].astype(F32)
    o_ig[...] = total.astype(BF16)

    sent("g", G)
    sent("p", PRE)
    sent("v", X.at[pl.ds(0, 7), 0])
    sent("w", X.at[pl.ds(0, 4)])
    sent("e", ES.at[pl.ds(0, 15)])
    sent("h", HG.at[pl.ds(0, 7)])
    sent("r", rs_s.at[pl.ds(0, 6)])
    sent("l", rl_s)
    sent("c", IGR)
    assert len(names) <= SEMS, len(names)


def hand_over(*refs):
    ins, outs, sems = refs[:4], refs[4:8], refs[8]
    copies = [pltpu.make_async_copy(a, b, sems.at[i]) for i, (a, b) in enumerate(zip(ins, outs))]
    for c in copies:
        c.start()
    for c in copies:
        c.wait()


def per_device(inputs, grad_out, gate_pre, up_pre, gate_weight, up_weight, down_weight):
    scale = 1.0 / math.sqrt(grad_out.shape[0] * lax.axis_size("row"))
    vm = pltpu.VMEM
    anywhere = pl.BlockSpec(memory_space=pl.ANY)
    shapes = (
        jax.ShapeDtypeStruct((32, 512), BF16),
        jax.ShapeDtypeStruct((512, 512), BF16),
        jax.ShapeDtypeStruct((512, 512), BF16),
        jax.ShapeDtypeStruct((512, 512), BF16),
    )
    parts = pl.pallas_call(
        functools.partial(kernel, scale),
        out_shape=tuple(vm(a.shape, a.dtype) for a in shapes),
        in_specs=[anywhere] * 7,
        out_specs=[pl.BlockSpec(memory_space=vm)] * 4,
        scratch_shapes=[
            vm((8, 2, 2, 32, 512), BF16),
            vm((8, 2, 2, 32, 512), BF16),
            vm((2, 8, 2, 64, 512), BF16),
            vm((8, 128, 512), F32),
            vm((8, 128, 512), F32),
            vm((512, 1024), BF16),
            vm((512, 1024), BF16),
            vm((512, 512), BF16),
            vm((512, 512), BF16),
            vm((512, 512), BF16),
            vm((8, 128, 512), F32),
            vm((8, 4, 128, 128), BF16),
            vm((8, 4, 128, 128), BF16),
            vm((4, 128, 128), F32),
            vm((4, 128, 128), F32),
            vm((4, 128, 128), BF16),
            vm((4, 128, 128), BF16),
            vm((4, 128, 128), F32),
            vm((8, 4, 128, 128), BF16),
            vm((8, 128, 512), BF16),
            vm((8, 128, 512), BF16),
            vm((8, 2, 2, 32, 512), F32),
            vm((8, 2, 32, 512), F32),
            vm((16, 32, 512), BF16),
            vm((16, 32, 512), BF16),
            vm((32, 512), F32),
            vm((512, 512), BF16),
            vm((512, 512), BF16),
            vm((512, 512), BF16),
            pltpu.SemaphoreType.DMA((9,)),
            pltpu.SemaphoreType.DMA((SEMS,)),
            pltpu.SemaphoreType.DMA((7,)),
        ],
        compiler_params=pltpu.CompilerParams(
            collective_id=0, has_side_effects=True, vmem_limit_bytes=56 * 1024 * 1024
        ),
        name="swiglu_backward",
    )(inputs, grad_out, gate_pre, up_pre, gate_weight, up_weight, down_weight)
    return pl.pallas_call(
        hand_over,
        out_shape=shapes,
        in_specs=[pl.BlockSpec(memory_space=vm)] * 4,
        out_specs=[anywhere] * 4,
        scratch_shapes=[pltpu.SemaphoreType.DMA((4,))],
        name="hand_over",
    )(*[pltpu.with_memory_space_constraint(p, pltpu.VMEM) for p in parts])


def solution(mesh):
    return jax.shard_map(
        per_device,
        mesh=mesh,
        in_specs=(
            P("row", "col"),
            P("row", "col"),
            P("col", "row"),
            P("col", "row"),
            P("col", "row"),
            P("col", "row"),
            P("row", "col"),
        ),
        out_specs=(P("row", "col"), P("col", "row"), P("col", "row"), P("row", "col")),
        check_vma=False,
    )
```

```python
import functools
import math

import jax
import jax.numpy as jnp
from jax import lax
from jax.experimental import pallas as pl
from jax.experimental.pallas import tpu as pltpu
from jax.sharding import PartitionSpec as P

MESH = pl.DeviceIdType.MESH
F32 = jnp.float32
BF16 = jnp.bfloat16
SEMS = 124


def mod8(v):
    return lax.rem(v + 16, 8)


def kernel(
    scale, inp, gout, gpre, upre, gw, uw, dw,
    o_ig, o_gg, o_ug, o_dg,
    G, X, PRE, A, B, HT, XT, dwt, gwt, uwt, PH, rs_s, rs_r, rl_s, rl_r, xs, xr, S,
    HG, TG, TU, IG, IGR, ES, ER, ACC, vgw, vuw, vdw, ss, rs, ls,
):
    col = lax.axis_index("col")
    row = lax.axis_index("row")
    z, xl = lax.div(col, 2), lax.rem(col, 2)
    y, xh, co = lax.div(row, 4), lax.rem(lax.div(row, 2), 2), lax.rem(row, 2)

    def at_z(zz):
        return {"col": zz * 2 + xl, "row": row}

    def at_y(yy, x=None):
        return {"col": col, "row": yy * 4 + (xh if x is None else x) * 2 + co}

    zdev = {1: at_z(mod8(z + 1)), -1: at_z(mod8(z - 1))}
    xlo = {"col": z * 2 + 1 - xl, "row": row}
    xhi = at_y(y, 1 - xh)
    sib = {"col": col, "row": y * 4 + xh * 2 + 1 - co}

    names = {}

    def sem(name):
        return names.setdefault(name, len(names))

    def copy(src, dst, i, j, dev):
        return pltpu.make_async_remote_copy(
            src_ref=src, dst_ref=dst, send_sem=ss.at[i], recv_sem=rs.at[j],
            device_id=dev, device_id_type=MESH,
        )

    groups = {"g": 0, "x": 0, "p": 1, "s": 1, "v": 2, "w": 3, "e": 4, "h": 5, "r": 6, "l": 7, "c": 8}

    def send(name, src, dst, dev):
        copy(src, dst, groups[name[0]], sem(name), dev).start()

    def sent(group, ref):
        i = groups[group]
        copy(ref, ref, i, 0, sib).wait_send()

    def recv_at(i, dst):
        copy(dst, dst, i, i, sib).wait_recv()

    def recv(name, dst):
        recv_at(sem(name), dst)

    bar = pltpu.get_barrier_semaphore()
    across = {"col": col, "row": y * 4 + (1 - xh) * 2 + 1 - co}
    partners = [zdev[1], zdev[-1], xlo, xhi, sib, across]
    partners += [at_y(mod8(y + d)) for d in range(1, 8)]
    partners += [at_y(mod8(y + d), 1 - xh) for d in range(1, 8)]
    for dev in partners:
        pl.semaphore_signal(bar, inc=1, device_id=dev, device_id_type=MESH)
    loads = [
        pltpu.make_async_copy(a, b, ls.at[i])
        for i, (a, b) in enumerate(
            (
                (gout, G.at[y, xh, co]),
                (gpre, PRE.at[0, z, xl]),
                (upre, PRE.at[1, z, xl]),
                (inp, X.at[y, xh, co]),
                (dw, vdw),
                (gw, vgw),
                (uw, vuw),
            )
        )
    ]
    for c in loads:
        c.start()
    pl.semaphore_wait(bar, len(partners))
    for c in loads[:4]:
        c.wait()

    yorder = [4, 3, 5, 2, 6, 1, 7]
    need = [4, 3, -3, 2, -2, 1, -1, 0]
    first = [4, 3, -3]
    own = G.at[y, xh, co]
    g0 = [sem(f"gy{d}") for d in range(8)][0]
    for d in yorder:
        send(f"gy{d}", own, own, at_y(mod8(y + d)))

    def pre_hops(a, s):
        return 4 if (a == 0) == (s == 1) else 3

    def pre_send(a, s, k):
        blk = PRE.at[a, mod8(z - s * (k - 1)), xl]
        send(f"pz{a}{s}{k}", blk, blk, zdev[s])

    def pre_x(d):
        blk = PRE.at[:, mod8(z + d), xl]
        send(f"px{d}", blk, blk, xlo)

    def pre_hop(k, get=True, put=True):
        for a in (0, 1):
            for s in (1, -1):
                if get and k <= pre_hops(a, s):
                    recv(f"pz{a}{s}{k}", PRE.at[a, mod8(z - s * k), xl])
                if put and k < pre_hops(a, s):
                    pre_send(a, s, k + 1)

    for a in (0, 1):
        for s in (1, -1):
            pre_send(a, s, 1)

    def g_row(j):
        t = mod8(z + j)
        d = mod8(y - t)

        @pl.when(d != 0)
        def _():
            recv_at(g0 + d, G.at[t, xh, co])

        blk = G.at[t, xh, co]
        send(f"gx{j}", blk, blk, xhi)
        if j in first:
            send(f"gz{j}", blk, blk, across)
            send(f"gs{j}", blk, blk, sib)

    def g_sib(j):
        if j in first:
            return
        t = mod8(z + j)
        recv(f"gx{j}", G.at[t, 1 - xh, co])
        blk = G.at[t, :, co]
        send(f"gs{j}", blk, blk, sib)

    def partial(j):
        t = mod8(z + j)
        if j in first:
            recv(f"gs{j}", G.at[t, xh, 1 - co])
            recv(f"gx{j}", G.at[t, 1 - xh, co])
            recv(f"gz{j}", G.at[t, 1 - xh, 1 - co])
        else:
            recv(f"gs{j}", G.at[t, :, 1 - co])
        PH[t] = jnp.dot(G[t].reshape(128, 512), dwt[...], preferred_element_type=F32)

    xown = X.at[y, xh, co]
    send("xx", xown, xown, xhi)
    pre_x(0)
    for c, v, t in zip(loads[4:], (vdw, vgw, vuw), (dwt, gwt, uwt)):
        c.wait()
        t[...] = v[...].T
    pre_hop(1)
    other = PRE.at[:, z, 1 - xl]
    recv("px0", other)
    for s in (1, -1):
        send(f"py{s}", other, other, zdev[s])
    for j in need[:5]:
        g_row(j)
    pre_hop(2)
    for j in need[:3]:
        g_sib(j)

    slices = [0, 1, 2, 3]

    def hops(q, s):
        return 4 if (q < 2) == (s == 1) else 3

    mixed = [0, 2, 1, 3]
    streams = [(q, s) for n in (4, 3) for q in mixed for s in (1, -1) if hops(q, s) == n]

    def cols(q):
        return pl.ds(q * 128, 128)

    def rs_step(q, s, k):
        n = hops(q, s)
        i = streams.index((q, s))
        t = mod8(z + s * (n - k + 1))
        val = PH[t, :, cols(q)]
        if k > 1:
            recv(f"r{i}{k - 1}", rs_r.at[i, k - 1])
            val = val + rs_r[i, k - 1].astype(F32)
        if k == 4:
            rl_s[i] = val
            send(f"l{i}", rl_s.at[i], rl_r.at[i], zdev[s])
        else:
            rs_s[i, k] = val.astype(BF16)
            send(f"r{i}{k}", rs_s.at[i, k], rs_r.at[i, k], zdev[s])

    def rs_all(n, k):
        for q, s in streams:
            if hops(q, s) == n:
                rs_step(q, s, k)

    def tokens(t):
        return pl.ds(pl.multiple_of(t * 128, 128), 128)

    def terms(j):
        t = mod8(z + j)
        if j:
            recv(f"py{-j}" if j in (1, -1) else f"px{j}", PRE.at[:, t, 1 - xl])
        for h in (0, 1):
            c = pl.ds(h * 256, 256)
            g = PRE[0, t, :, :, c].reshape(128, 256).astype(F32)
            u = PRE[1, t, :, :, c].reshape(128, 256).astype(F32)
            sg = 1.0 / (1.0 + jnp.exp(-g))
            silu = g * sg
            A[t, :, c] = silu
            HT[c, tokens(t)] = (silu * u).astype(BF16).T
            B[t, :, c] = u * sg * (1.0 + g * (1.0 - sg))

    partial(4)
    rs_all(4, 1)
    for j in need[5:]:
        g_row(j)
    partial(3)
    partial(-3)
    rs_all(3, 1)
    pre_x(-2)
    pre_x(2)
    g_sib(2)
    g_sib(-2)
    rs_all(4, 2)
    partial(2)
    partial(-2)
    rs_all(3, 2)
    for j in (1, -1, 0):
        g_sib(j)
    recv("xx", X.at[y, 1 - xh, co])
    xpair = X.at[y, :, co]
    for d in yorder:
        copy(xpair, xpair, groups["v"], sem("v"), at_y(mod8(y + d))).start()
    rs_all(4, 3)
    partial(1)
    partial(-1)
    pre_hop(3, put=False)
    pre_x(-3)
    pre_x(3)
    rs_all(3, 3)
    terms(0)
    rs_all(4, 4)
    partial(0)
    pre_hop(3, get=False)
    terms(-1)
    terms(1)
    for q in mixed:
        val = PH[z, :, cols(q)]
        for s in (1, -1):
            n = hops(q, s)
            i = streams.index((q, s))
            if n == 4:
                recv(f"l{i}", rl_r.at[i])
                val = val + rl_r[i]
            else:
                recv(f"r{i}{n}", rs_r.at[i, n])
                val = val + rs_r[i, n].astype(F32)
        S[q] = val
        xs[q] = val.astype(BF16)
        send(f"s{q}", xs.at[q], xr.at[q], xlo)

    def hg_send(q, s, k):
        blk = HG.at[mod8(z - s * (k - 1)), q]
        send(f"h{streams.index((q, s))}{k}", blk, blk, zdev[s])

    for q in mixed:
        recv(f"s{q}", xr.at[q])
        HG[z, q] = (S[q] + xr[q].astype(F32)).astype(BF16)
        hg_send(q, 1, 1)
        hg_send(q, -1, 1)

    def block(slot, j):
        t = mod8(z + j)
        for q in slices:
            hg = HG[t, q].astype(F32)
            TG[t, :, cols(q)] = (hg * B[t, :, cols(q)]).astype(BF16)
            TU[t, :, cols(q)] = (hg * A[t, :, cols(q)]).astype(BF16)
        val = jnp.dot(TG[t], gwt[...], preferred_element_type=F32) + jnp.dot(
            TU[t], uwt[...], preferred_element_type=F32
        )
        IG[slot] = val.reshape(2, 2, 32, 512)
        send(f"c{slot}", IG.at[slot, :, 1 - co], IGR.at[slot], sib)


    def e_copy(slot, j, other):
        t = mod8(z + j)
        d = mod8(t - y)
        return copy(
            ES.at[8 * other + slot], ER.at[8 * other + d], groups["e"], sem("e"),
            at_y(t, 1 - xh if other else xh),
        )

    def out_block(slot, j):
        t = mod8(z + j)
        recv(f"c{slot}", IGR.at[slot])
        ES[8 + slot] = (IG[slot, 1 - xh, co] + IGR[slot, 1 - xh]).astype(BF16)
        e_copy(slot, j, 1).start()
        val = IG[slot, xh, co] + IGR[slot, xh]

        @pl.when(t == y)
        def _():
            ACC[...] = val

        @pl.when(t != y)
        def _():
            ES[slot] = val.astype(BF16)
            e_copy(slot, j, 0).start()

    order = [0, -1, 1, -2, 2, -3, 3, 4]

    def grad(lhs, rhs, out):
        def body(n, carry):
            rows = pl.ds(pl.multiple_of(n * 256, 256), 256)
            acc = jnp.dot(lhs[rows, :], rhs[...].reshape(1024, 512), preferred_element_type=F32)
            out[rows, :] = (acc * scale).astype(BF16)
            return carry

        lax.fori_loop(0, 2, body, 0)

    def hop(n, k):
        for q, s in streams:
            if hops(q, s) == n:
                recv(f"h{streams.index((q, s))}{k}", HG.at[mod8(z - s * k), q])
                if k < n:
                    hg_send(q, s, k + 1)

    def blocks(*js):
        for j in js:
            block(order.index(j), j)

    def outs(*js):
        for j in js:
            out_block(order.index(j), j)

    blocks(0)
    hop(4, 1)
    terms(-2)
    terms(2)
    outs(0)
    hop(3, 1)
    pre_hop(4)
    pre_x(4)
    blocks(-1, 1)
    recv("v", X.at[pl.ds(0, 7), 0])
    send("w", X.at[:, :, co], X.at[:, :, co], sib)
    hop(4, 2)
    outs(-1, 1)
    hop(3, 2)
    blocks(-2, 2)
    recv("w", X.at[:, :, 1 - co])
    for t in range(8):
        XT[:, t * 128 : t * 128 + 128] = X[t].reshape(128, 512).T
    hop(4, 3)
    outs(-2, 2)
    hop(3, 3)
    terms(-3)
    terms(3)
    blocks(-3, 3)
    terms(4)
    outs(-3, 3)
    hop(4, 4)
    blocks(4)
    outs(4)

    grad(HT, G, o_dg)
    grad(XT, TG, o_gg)
    grad(XT, TU, o_ug)
    recv("e", ER.at[pl.ds(1, 15)])
    total = ACC[...]
    for i in range(1, 16):
        total = total + ER[i].astype(F32)
    o_ig[...] = total.astype(BF16)

    sent("g", G)
    sent("p", PRE)
    sent("v", X.at[pl.ds(0, 7), 0])
    sent("w", X.at[pl.ds(0, 4)])
    sent("e", ES.at[pl.ds(0, 15)])
    sent("h", HG.at[pl.ds(0, 7)])
    sent("r", rs_s.at[pl.ds(0, 6)])
    sent("l", rl_s)
    sent("c", IGR)
    assert len(names) <= SEMS, len(names)


def hand_over(*refs):
    ins, outs, sems = refs[:4], refs[4:8], refs[8]
    copies = [pltpu.make_async_copy(a, b, sems.at[i]) for i, (a, b) in enumerate(zip(ins, outs))]
    for c in copies:
        c.start()
    for c in copies:
        c.wait()


def per_device(inputs, grad_out, gate_pre, up_pre, gate_weight, up_weight, down_weight):
    scale = 1.0 / math.sqrt(grad_out.shape[0] * lax.axis_size("row"))
    vm = pltpu.VMEM
    anywhere = pl.BlockSpec(memory_space=pl.ANY)
    shapes = (
        jax.ShapeDtypeStruct((32, 512), BF16),
        jax.ShapeDtypeStruct((512, 512), BF16),
        jax.ShapeDtypeStruct((512, 512), BF16),
        jax.ShapeDtypeStruct((512, 512), BF16),
    )
    parts = pl.pallas_call(
        functools.partial(kernel, scale),
        out_shape=tuple(vm(a.shape, a.dtype) for a in shapes),
        in_specs=[anywhere] * 7,
        out_specs=[pl.BlockSpec(memory_space=vm)] * 4,
        scratch_shapes=[
            vm((8, 2, 2, 32, 512), BF16),
            vm((8, 2, 2, 32, 512), BF16),
            vm((2, 8, 2, 64, 512), BF16),
            vm((8, 128, 512), F32),
            vm((8, 128, 512), F32),
            vm((512, 1024), BF16),
            vm((512, 1024), BF16),
            vm((512, 512), BF16),
            vm((512, 512), BF16),
            vm((512, 512), BF16),
            vm((8, 128, 512), F32),
            vm((8, 4, 128, 128), BF16),
            vm((8, 4, 128, 128), BF16),
            vm((4, 128, 128), F32),
            vm((4, 128, 128), F32),
            vm((4, 128, 128), BF16),
            vm((4, 128, 128), BF16),
            vm((4, 128, 128), F32),
            vm((8, 4, 128, 128), BF16),
            vm((8, 128, 512), BF16),
            vm((8, 128, 512), BF16),
            vm((8, 2, 2, 32, 512), F32),
            vm((8, 2, 32, 512), F32),
            vm((16, 32, 512), BF16),
            vm((16, 32, 512), BF16),
            vm((32, 512), F32),
            vm((512, 512), BF16),
            vm((512, 512), BF16),
            vm((512, 512), BF16),
            pltpu.SemaphoreType.DMA((9,)),
            pltpu.SemaphoreType.DMA((SEMS,)),
            pltpu.SemaphoreType.DMA((7,)),
        ],
        compiler_params=pltpu.CompilerParams(
            collective_id=0, has_side_effects=True, vmem_limit_bytes=56 * 1024 * 1024
        ),
        name="swiglu_backward",
    )(inputs, grad_out, gate_pre, up_pre, gate_weight, up_weight, down_weight)
    return pl.pallas_call(
        hand_over,
        out_shape=shapes,
        in_specs=[pl.BlockSpec(memory_space=vm)] * 4,
        out_specs=[anywhere] * 4,
        scratch_shapes=[pltpu.SemaphoreType.DMA((4,))],
        name="hand_over",
    )(*[pltpu.with_memory_space_constraint(p, pltpu.VMEM) for p in parts])


def solution(mesh):
    return jax.shard_map(
        per_device,
        mesh=mesh,
        in_specs=(
            P("row", "col"),
            P("row", "col"),
            P("col", "row"),
            P("col", "row"),
            P("col", "row"),
            P("col", "row"),
            P("row", "col"),
        ),
        out_specs=(P("row", "col"), P("col", "row"), P("col", "row"), P("row", "col")),
        check_vma=False,
    )
```

```python
import functools
import math

import jax
import jax.numpy as jnp
from jax import lax
from jax.experimental import pallas as pl
from jax.experimental.pallas import tpu as pltpu
from jax.sharding import PartitionSpec as P

MESH = pl.DeviceIdType.MESH
F32 = jnp.float32
BF16 = jnp.bfloat16
SEMS = 124


def mod8(v):
    return lax.rem(v + 16, 8)


def kernel(
    scale, inp, gout, gpre, upre, gw, uw, dw,
    o_ig, o_gg, o_ug, o_dg,
    G, X, PRE, A, B, HT, XT, dwt, gwt, uwt, PH, rs_s, rs_r, rl_s, rl_r, xs, xr, S,
    HG, TG, TU, IG, IGR, ES, ER, ACC, vgw, vuw, vdw, ss, rs, ls,
):
    col = lax.axis_index("col")
    row = lax.axis_index("row")
    z, xl = lax.div(col, 2), lax.rem(col, 2)
    y, xh, co = lax.div(row, 4), lax.rem(lax.div(row, 2), 2), lax.rem(row, 2)

    def at_z(zz):
        return {"col": zz * 2 + xl, "row": row}

    def at_y(yy, x=None):
        return {"col": col, "row": yy * 4 + (xh if x is None else x) * 2 + co}

    zdev = {1: at_z(mod8(z + 1)), -1: at_z(mod8(z - 1))}
    xlo = {"col": z * 2 + 1 - xl, "row": row}
    xhi = at_y(y, 1 - xh)
    sib = {"col": col, "row": y * 4 + xh * 2 + 1 - co}

    names = {}

    def sem(name):
        return names.setdefault(name, len(names))

    def copy(src, dst, i, j, dev):
        return pltpu.make_async_remote_copy(
            src_ref=src, dst_ref=dst, send_sem=ss.at[i], recv_sem=rs.at[j],
            device_id=dev, device_id_type=MESH,
        )

    groups = {"g": 0, "x": 0, "p": 1, "s": 1, "v": 2, "w": 3, "e": 4, "h": 5, "r": 6, "l": 7, "c": 8}

    def send(name, src, dst, dev):
        copy(src, dst, groups[name[0]], sem(name), dev).start()

    def sent(group, ref):
        i = groups[group]
        copy(ref, ref, i, 0, sib).wait_send()

    def recv_at(i, dst):
        copy(dst, dst, i, i, sib).wait_recv()

    def recv(name, dst):
        recv_at(sem(name), dst)

    bar = pltpu.get_barrier_semaphore()
    across = {"col": col, "row": y * 4 + (1 - xh) * 2 + 1 - co}
    partners = [zdev[1], zdev[-1], xlo, xhi, sib, across]
    partners += [at_y(mod8(y + d)) for d in range(1, 8)]
    partners += [at_y(mod8(y + d), 1 - xh) for d in range(1, 8)]
    for dev in partners:
        pl.semaphore_signal(bar, inc=1, device_id=dev, device_id_type=MESH)
    loads = [
        pltpu.make_async_copy(a, b, ls.at[i])
        for i, (a, b) in enumerate(
            (
                (gout, G.at[y, xh, co]),
                (gpre, PRE.at[0, z, xl]),
                (upre, PRE.at[1, z, xl]),
                (inp, X.at[y, xh, co]),
                (dw, vdw),
                (gw, vgw),
                (uw, vuw),
            )
        )
    ]
    for c in loads:
        c.start()
    pl.semaphore_wait(bar, len(partners))
    for c in loads[:4]:
        c.wait()

    yorder = [4, 3, 5, 2, 6, 1, 7]
    need = [4, 3, -3, 2, -2, 1, -1, 0]
    first = [4, 3, -3]
    own = G.at[y, xh, co]
    g0 = [sem(f"gy{d}") for d in range(8)][0]
    for d in yorder:
        send(f"gy{d}", own, own, at_y(mod8(y + d)))

    def pre_hops(a, s):
        return 4 if (a == 0) == (s == 1) else 3

    def pre_send(a, s, k):
        blk = PRE.at[a, mod8(z - s * (k - 1)), xl]
        send(f"pz{a}{s}{k}", blk, blk, zdev[s])

    def pre_x(d):
        blk = PRE.at[:, mod8(z + d), xl]
        send(f"px{d}", blk, blk, xlo)

    def pre_hop(k, get=True, put=True):
        for a in (0, 1):
            for s in (1, -1):
                if get and k <= pre_hops(a, s):
                    recv(f"pz{a}{s}{k}", PRE.at[a, mod8(z - s * k), xl])
                if put and k < pre_hops(a, s):
                    pre_send(a, s, k + 1)

    for a in (0, 1):
        for s in (1, -1):
            pre_send(a, s, 1)

    def g_row(j):
        t = mod8(z + j)
        d = mod8(y - t)

        @pl.when(d != 0)
        def _():
            recv_at(g0 + d, G.at[t, xh, co])

        blk = G.at[t, xh, co]
        send(f"gx{j}", blk, blk, xhi)
        if j in first:
            send(f"gz{j}", blk, blk, across)
            send(f"gs{j}", blk, blk, sib)

    def g_sib(j):
        if j in first:
            return
        t = mod8(z + j)
        recv(f"gx{j}", G.at[t, 1 - xh, co])
        blk = G.at[t, :, co]
        send(f"gs{j}", blk, blk, sib)

    def partial(j):
        t = mod8(z + j)
        if j in first:
            recv(f"gs{j}", G.at[t, xh, 1 - co])
            recv(f"gx{j}", G.at[t, 1 - xh, co])
            recv(f"gz{j}", G.at[t, 1 - xh, 1 - co])
        else:
            recv(f"gs{j}", G.at[t, :, 1 - co])
        PH[t] = jnp.dot(G[t].reshape(128, 512), dwt[...], preferred_element_type=F32)

    xown = X.at[y, xh, co]
    send("xx", xown, xown, xhi)
    pre_x(0)
    for c, v, t in zip(loads[4:], (vdw, vgw, vuw), (dwt, gwt, uwt)):
        c.wait()
        t[...] = v[...].T
    pre_hop(1)
    other = PRE.at[:, z, 1 - xl]
    recv("px0", other)
    for s in (1, -1):
        send(f"py{s}", other, other, zdev[s])
    for j in need[:5]:
        g_row(j)
    pre_hop(2)
    for j in need[:3]:
        g_sib(j)

    slices = [0, 1, 2, 3]

    def hops(q, s):
        return 4 if (q < 2) == (s == 1) else 3

    mixed = [0, 2, 1, 3]
    streams = [(q, s) for n in (4, 3) for q in mixed for s in (1, -1) if hops(q, s) == n]

    def cols(q):
        return pl.ds(q * 128, 128)

    def rs_step(q, s, k):
        n = hops(q, s)
        i = streams.index((q, s))
        t = mod8(z + s * (n - k + 1))
        val = PH[t, :, cols(q)]
        if k > 1:
            recv(f"r{i}{k - 1}", rs_r.at[i, k - 1])
            val = val + rs_r[i, k - 1].astype(F32)
        if k == 4:
            rl_s[i] = val
            send(f"l{i}", rl_s.at[i], rl_r.at[i], zdev[s])
        else:
            rs_s[i, k] = val.astype(BF16)
            send(f"r{i}{k}", rs_s.at[i, k], rs_r.at[i, k], zdev[s])

    def rs_all(n, k):
        for q, s in streams:
            if hops(q, s) == n:
                rs_step(q, s, k)

    def tokens(t):
        return pl.ds(pl.multiple_of(t * 128, 128), 128)

    def terms(j):
        t = mod8(z + j)
        if j:
            recv(f"py{-j}" if j in (1, -1) else f"px{j}", PRE.at[:, t, 1 - xl])
        for h in (0, 1):
            c = pl.ds(h * 256, 256)
            g = PRE[0, t, :, :, c].reshape(128, 256).astype(F32)
            u = PRE[1, t, :, :, c].reshape(128, 256).astype(F32)
            sg = 1.0 / (1.0 + jnp.exp(-g))
            silu = g * sg
            A[t, :, c] = silu
            HT[c, tokens(t)] = (silu * u).astype(BF16).T
            B[t, :, c] = u * sg * (1.0 + g * (1.0 - sg))

    partial(4)
    rs_all(4, 1)
    for j in need[5:]:
        g_row(j)
    partial(3)
    partial(-3)
    rs_all(3, 1)
    pre_x(-2)
    pre_x(2)
    g_sib(2)
    g_sib(-2)
    rs_all(4, 2)
    partial(2)
    partial(-2)
    rs_all(3, 2)
    for j in (1, -1, 0):
        g_sib(j)
    pre_hop(3, put=False)
    pre_x(-3)
    pre_x(3)
    recv("xx", X.at[y, 1 - xh, co])
    xpair = X.at[y, :, co]
    for d in yorder:
        copy(xpair, xpair, groups["v"], sem("v"), at_y(mod8(y + d))).start()
    rs_all(4, 3)
    partial(1)
    partial(-1)
    rs_all(3, 3)
    terms(0)
    rs_all(4, 4)
    partial(0)
    pre_hop(3, get=False)
    terms(-1)
    terms(1)
    for q in mixed:
        val = PH[z, :, cols(q)]
        for s in (1, -1):
            n = hops(q, s)
            i = streams.index((q, s))
            if n == 4:
                recv(f"l{i}", rl_r.at[i])
                val = val + rl_r[i]
            else:
                recv(f"r{i}{n}", rs_r.at[i, n])
                val = val + rs_r[i, n].astype(F32)
        S[q] = val
        xs[q] = val.astype(BF16)
        send(f"s{q}", xs.at[q], xr.at[q], xlo)

    def hg_send(q, s, k):
        blk = HG.at[mod8(z - s * (k - 1)), q]
        send(f"h{streams.index((q, s))}{k}", blk, blk, zdev[s])

    for q in mixed:
        recv(f"s{q}", xr.at[q])
        HG[z, q] = (S[q] + xr[q].astype(F32)).astype(BF16)
        hg_send(q, 1, 1)
        hg_send(q, -1, 1)

    def block(slot, j):
        t = mod8(z + j)
        for q in slices:
            hg = HG[t, q].astype(F32)
            TG[t, :, cols(q)] = (hg * B[t, :, cols(q)]).astype(BF16)
            TU[t, :, cols(q)] = (hg * A[t, :, cols(q)]).astype(BF16)
        val = jnp.dot(TG[t], gwt[...], preferred_element_type=F32) + jnp.dot(
            TU[t], uwt[...], preferred_element_type=F32
        )
        IG[slot] = val.reshape(2, 2, 32, 512)
        send(f"c{slot}", IG.at[slot, :, 1 - co], IGR.at[slot], sib)


    def e_copy(slot, j, other):
        t = mod8(z + j)
        d = mod8(t - y)
        return copy(
            ES.at[8 * other + slot], ER.at[8 * other + d], groups["e"], sem("e"),
            at_y(t, 1 - xh if other else xh),
        )

    def out_block(slot, j):
        t = mod8(z + j)
        recv(f"c{slot}", IGR.at[slot])
        ES[8 + slot] = (IG[slot, 1 - xh, co] + IGR[slot, 1 - xh]).astype(BF16)
        e_copy(slot, j, 1).start()
        val = IG[slot, xh, co] + IGR[slot, xh]

        @pl.when(t == y)
        def _():
            ACC[...] = val

        @pl.when(t != y)
        def _():
            ES[slot] = val.astype(BF16)
            e_copy(slot, j, 0).start()

    order = [0, -1, 1, -2, 2, -3, 3, 4]

    def grad(lhs, rhs, out):
        def body(n, carry):
            rows = pl.ds(pl.multiple_of(n * 256, 256), 256)
            acc = jnp.dot(lhs[rows, :], rhs[...].reshape(1024, 512), preferred_element_type=F32)
            out[rows, :] = (acc * scale).astype(BF16)
            return carry

        lax.fori_loop(0, 2, body, 0)

    def hop(n, k):
        for q, s in streams:
            if hops(q, s) == n:
                recv(f"h{streams.index((q, s))}{k}", HG.at[mod8(z - s * k), q])
                if k < n:
                    hg_send(q, s, k + 1)

    def blocks(*js):
        for j in js:
            block(order.index(j), j)

    def outs(*js):
        for j in js:
            out_block(order.index(j), j)

    blocks(0)
    hop(4, 1)
    terms(-2)
    terms(2)
    outs(0)
    hop(3, 1)
    pre_hop(4)
    pre_x(4)
    blocks(-1, 1)
    recv("v", X.at[pl.ds(0, 7), 0])
    send("w", X.at[:, :, co], X.at[:, :, co], sib)
    hop(4, 2)
    outs(-1, 1)
    hop(3, 2)
    blocks(-2, 2)
    recv("w", X.at[:, :, 1 - co])
    for t in range(8):
        XT[:, t * 128 : t * 128 + 128] = X[t].reshape(128, 512).T
    hop(4, 3)
    outs(-2, 2)
    hop(3, 3)
    terms(-3)
    terms(3)
    blocks(-3, 3)
    terms(4)
    outs(-3, 3)
    hop(4, 4)
    blocks(4)
    outs(4)

    grad(HT, G, o_dg)
    grad(XT, TG, o_gg)
    grad(XT, TU, o_ug)
    recv("e", ER.at[pl.ds(1, 15)])
    total = ACC[...]
    for i in range(1, 16):
        total = total + ER[i].astype(F32)
    o_ig[...] = total.astype(BF16)

    sent("g", G)
    sent("p", PRE)
    sent("v", X.at[pl.ds(0, 7), 0])
    sent("w", X.at[pl.ds(0, 4)])
    sent("e", ES.at[pl.ds(0, 15)])
    sent("h", HG.at[pl.ds(0, 7)])
    sent("r", rs_s.at[pl.ds(0, 6)])
    sent("l", rl_s)
    sent("c", IGR)
    assert len(names) <= SEMS, len(names)


def hand_over(*refs):
    ins, outs, sems = refs[:4], refs[4:8], refs[8]
    copies = [pltpu.make_async_copy(a, b, sems.at[i]) for i, (a, b) in enumerate(zip(ins, outs))]
    for c in copies:
        c.start()
    for c in copies:
        c.wait()


def per_device(inputs, grad_out, gate_pre, up_pre, gate_weight, up_weight, down_weight):
    scale = 1.0 / math.sqrt(grad_out.shape[0] * lax.axis_size("row"))
    vm = pltpu.VMEM
    anywhere = pl.BlockSpec(memory_space=pl.ANY)
    shapes = (
        jax.ShapeDtypeStruct((32, 512), BF16),
        jax.ShapeDtypeStruct((512, 512), BF16),
        jax.ShapeDtypeStruct((512, 512), BF16),
        jax.ShapeDtypeStruct((512, 512), BF16),
    )
    parts = pl.pallas_call(
        functools.partial(kernel, scale),
        out_shape=tuple(vm(a.shape, a.dtype) for a in shapes),
        in_specs=[anywhere] * 7,
        out_specs=[pl.BlockSpec(memory_space=vm)] * 4,
        scratch_shapes=[
            vm((8, 2, 2, 32, 512), BF16),
            vm((8, 2, 2, 32, 512), BF16),
            vm((2, 8, 2, 64, 512), BF16),
            vm((8, 128, 512), F32),
            vm((8, 128, 512), F32),
            vm((512, 1024), BF16),
            vm((512, 1024), BF16),
            vm((512, 512), BF16),
            vm((512, 512), BF16),
            vm((512, 512), BF16),
            vm((8, 128, 512), F32),
            vm((8, 4, 128, 128), BF16),
            vm((8, 4, 128, 128), BF16),
            vm((4, 128, 128), F32),
            vm((4, 128, 128), F32),
            vm((4, 128, 128), BF16),
            vm((4, 128, 128), BF16),
            vm((4, 128, 128), F32),
            vm((8, 4, 128, 128), BF16),
            vm((8, 128, 512), BF16),
            vm((8, 128, 512), BF16),
            vm((8, 2, 2, 32, 512), F32),
            vm((8, 2, 32, 512), F32),
            vm((16, 32, 512), BF16),
            vm((16, 32, 512), BF16),
            vm((32, 512), F32),
            vm((512, 512), BF16),
            vm((512, 512), BF16),
            vm((512, 512), BF16),
            pltpu.SemaphoreType.DMA((9,)),
            pltpu.SemaphoreType.DMA((SEMS,)),
            pltpu.SemaphoreType.DMA((7,)),
        ],
        compiler_params=pltpu.CompilerParams(
            collective_id=0, has_side_effects=True, vmem_limit_bytes=56 * 1024 * 1024
        ),
        name="swiglu_backward",
    )(inputs, grad_out, gate_pre, up_pre, gate_weight, up_weight, down_weight)
    return pl.pallas_call(
        hand_over,
        out_shape=shapes,
        in_specs=[pl.BlockSpec(memory_space=vm)] * 4,
        out_specs=[anywhere] * 4,
        scratch_shapes=[pltpu.SemaphoreType.DMA((4,))],
        name="hand_over",
    )(*[pltpu.with_memory_space_constraint(p, pltpu.VMEM) for p in parts])


def solution(mesh):
    return jax.shard_map(
        per_device,
        mesh=mesh,
        in_specs=(
            P("row", "col"),
            P("row", "col"),
            P("col", "row"),
            P("col", "row"),
            P("col", "row"),
            P("col", "row"),
            P("row", "col"),
        ),
        out_specs=(P("row", "col"), P("col", "row"), P("col", "row"), P("row", "col")),
        check_vma=False,
    )
```
